256 devices in a mesh: space: 128 (over x, y, z), rep: 2 (over core).
Axes of the slice: x: 4, y: 4, z: 8, core: 2. Of those that a mesh axis runs over, the one named last changes fastest.
Arguments:
- acts: bfloat16 [3072, 512, 128], P(('space', 'rep')), may hold values from -6 to 6
- preact: bfloat16 [3072, 512, 128], P(('space', 'rep')), may hold values from -8 to 8
- cotangent: bfloat16 [3072, 512, 128], P(('space', 'rep')), may hold values from -6 to 6
- filt: bfloat16 [3456, 128], P('space', 'rep'), may hold values from -0.109375 to 0.109375
- counts: int32 [256], replicated, may hold values from 1 to 12, as said below
- neighbors: int32 [3072, 27], P(('space', 'rep')), may hold values from 0 to 3072, as said below
Outputs:
- input_grad: bfloat16 [3072, 512, 128], P(('space', 'rep'))
- filt_grad: float32 [3456, 128], P('space', 'rep')
The draws below stay inside these ranges and needn't reach their ends.
Inputs may be any that keep to these rules, and one draw needn't show every extreme that they name: counts[d] is the number of live bricks of device d, which fill its first slots; counts[d] + counts[d xor 1] <= 16, where d xor 1 is the other core of the same chip; in every draw some device holds 12 bricks and its partner 2 * 8 - 12. Brick n = d * 12 + s sits in slab d of the brick grid at one of 5 x 5 places, slot 0 of every device at the middle place; neighbors[n, k] is the index of the live brick at offset off_k (first component along the slabs, so it lies on device d - 1, d or d + 1) from that place, or 3072 where there is none, also for bricks that are not live.
All inputs are finite; a program needn't handle non-finite values.
Results may differ from the reference program's by a relative error of at most 0.0049.
Values may be sent and summed in bfloat16 or wider, within the bound.
A program may use at most 128 MiB of HBM per device.

```python
import math
import jax
import jax.numpy as jnp
from jax import lax

C = 128
BRICK = 8
SIDE = 5
SLOTS = 12
KEEP = 8
VOX = 512
BRICKS = 3072


def brick_layout(key):
    devices = BRICKS // SLOTS
    halves = devices // 2
    base_key = jax.random.fold_in(key, 7)
    key_total, key_split, key_pinned, key_flip, key_perm = jax.random.split(base_key, 5)
    pair_index = jnp.arange(halves)
    pinned = jax.random.randint(key_pinned, (), 0, halves)
    pair_total = jax.random.randint(key_total, (halves,), 2, 2 * KEEP + 1)
    pair_total = jnp.where(pair_index == pinned, 2 * KEEP, pair_total)
    lowest = jnp.maximum(1, pair_total - SLOTS)
    highest = jnp.minimum(SLOTS, pair_total - 1)
    first_share = jax.random.randint(key_split, (halves,), lowest, highest + 1)
    first_share = jnp.where(pair_index == pinned, SLOTS, first_share)
    second = pair_total - first_share
    flipped = jax.random.randint(key_flip, (halves,), 0, 2) == 1
    low_part = jnp.where(flipped, second, first_share)
    high_part = jnp.where(flipped, first_share, second)
    counts = jnp.stack([low_part, high_part], axis=1).reshape(devices).astype(jnp.int32)
    middle = SIDE * SIDE // 2
    device_keys = jax.random.split(key_perm, devices)
    others = jax.vmap(lambda key_one: jax.random.permutation(key_one, SIDE * SIDE - 1))(device_keys).astype(jnp.int32)
    others = others + (others >= middle).astype(jnp.int32)
    places = jnp.concatenate([jnp.full((devices, 1), middle, jnp.int32), others], axis=1).astype(jnp.int32)
    occupant = jnp.zeros((devices, SIDE * SIDE), jnp.int32).at[jnp.arange(devices)[:, None], places].set(jnp.arange(SIDE * SIDE, dtype=jnp.int32)[None, :])
    placed = places[:, :SLOTS]
    taps = jnp.arange(27)
    step_x = taps // 9 - 1
    step_y = taps // 3 % 3 - 1
    step_z = taps % 3 - 1
    target_dev = jnp.arange(devices)[:, None, None] + step_x[None, None, :]
    target_row = placed[:, :, None] // SIDE + step_y[None, None, :]
    target_col = placed[:, :, None] % SIDE + step_z[None, None, :]
    inside = (target_dev >= 0) & (target_dev < devices) & (target_row >= 0) & (target_row < SIDE) & (target_col >= 0) & (target_col < SIDE)
    clipped_dev = jnp.clip(target_dev, 0, devices - 1)
    clipped_row = jnp.clip(target_row, 0, SIDE - 1)
    clipped_col = jnp.clip(target_col, 0, SIDE - 1)
    target_slot = occupant[clipped_dev, clipped_row * SIDE + clipped_col]
    alive = inside & (target_slot < counts[clipped_dev])
    neighbor_table = jnp.where(alive, clipped_dev * SLOTS + target_slot, BRICKS).astype(jnp.int32)
    return (counts, neighbor_table.reshape(BRICKS, 27))


def draw_counts(key, part):
    return brick_layout(key)[0]


def draw_neighbors(key, part):
    return brick_layout(key)[1]


def levels(key, extent, cuts, least, largest):
    def one(dim, blocks):
        steps = jax.random.uniform(jax.random.fold_in(jax.random.fold_in(key, 6), dim), (blocks,), jnp.float32, least / len(cuts), largest / len(cuts))
        return jnp.repeat(jnp.exp(steps), extent[dim] // blocks).reshape((-1,) + (1,) * (len(extent) - dim - 1))

    gain = one(*cuts[0])
    for cut in cuts[1:]:
        gain = gain * one(*cut)
    return gain


def scatter_about(stream_key, extent, scale, most, pieces=(), kind=jnp.bfloat16):
    factor_of = levels(stream_key, extent, pieces, -0.22, 0.18) if pieces else 1.0
    drawn = jax.random.normal(stream_key, extent, jnp.float32) * scale * factor_of
    return jnp.minimum(jnp.maximum(drawn, -most), most).astype(kind)


def setup_inputs(seed: int = 0) -> dict:
    key_of = jax.random.split(jax.random.key(seed), 7)
    acts = scatter_about(key_of[0], (BRICKS, VOX, C), 1.0, 6.0, ((0, 256),))
    preact = scatter_about(key_of[1], (BRICKS, VOX, C), 1.5, 8.0, ((0, 256),))
    cotangent = scatter_about(key_of[2], (BRICKS, VOX, C), 1.0, 6.0, ((0, 256),))
    filt = scatter_about(key_of[3], (27 * C, C), (27 * C) ** -0.5, 0.109375, ((0, 128), (1, 2)))
    counts = draw_counts(jax.random.fold_in(key_of[6], 71), 0)
    neighbors = draw_neighbors(jax.random.fold_in(key_of[6], 71), 0)
    return {"acts": acts, "preact": preact, "cotangent": cotangent, "filt": filt, "counts": counts, "neighbors": neighbors}


tap_offsets = [(step_x, step_y, step_z) for step_x in (-1, 0, 1) for step_y in (-1, 0, 1) for step_z in (-1, 0, 1)]

def silu_slope(values):
    sigma = jax.nn.sigmoid(values)
    return sigma * (1.0 + values * (1.0 - sigma))

def edge(offset, brick_side):
    if offset < 0:
        return slice(brick_side - 1, brick_side)
    if offset == 0:
        return slice(0, brick_side)
    return slice(0, 1)

def assemble(planes, indices, usable):
    layers = []
    for step_x in range(3):
        strips = []
        for step_y in range(3):
            columns = []
            for step_z in range(3):
                tap = step_x * 9 + step_y * 3 + step_z
                source = planes[step_x]
                brick_side = source.shape[2]
                fetched = jnp.take(source, indices[:, tap], axis=0)
                fetched = fetched[:, :, edge(step_y - 1, brick_side), edge(step_z - 1, brick_side)]
                keeper = usable[:, tap][:, None, None, None, None]
                columns.append(jnp.where(keeper, fetched, jnp.zeros_like(fetched)))
            strips.append(jnp.concatenate(columns, axis=3))
        layers.append(jnp.concatenate(strips, axis=2))
    return jnp.concatenate(layers, axis=1)

def unfold(padded, direction):
    brick_side = padded.shape[0] - 2
    sections = []
    for step_x, step_y, step_z in tap_offsets:
        start_x = 1 + direction * step_x
        start_y = 1 + direction * step_y
        start_z = 1 + direction * step_z
        sections.append(padded[start_x:start_x + brick_side, start_y:start_y + brick_side, start_z:start_z + brick_side])
    return jnp.concatenate(sections, axis=-1).reshape(brick_side ** 3, -1)

def run_bricks(act_pad, grad_pad, filt_flip, running):

    def per_brick(accum, operands):
        act_block, grad_block = operands
        unrolled_act = unfold(act_block, 1)
        unrolled_grad = unfold(grad_block, -1)
        center = grad_block[1:-1, 1:-1, 1:-1].reshape(-1, grad_block.shape[-1])
        accum = accum + lax.dot_general(unrolled_act, center, (((0,), (0,)), ((), ())), preferred_element_type=jnp.float32)
        return (accum, jnp.dot(unrolled_grad, filt_flip, preferred_element_type=jnp.float32))
    return lax.scan(per_brick, running, (act_pad, grad_pad))

def reference(acts, preact, cotangent, filt, counts, neighbors):
    channels = acts.shape[2]
    devices = BRICKS // SLOTS
    is_live = jnp.arange(BRICKS) % SLOTS < jnp.repeat(counts, SLOTS)
    grad_pre = jnp.where(is_live[:, None, None], cotangent.astype(jnp.float32) * silu_slope(preact.astype(jnp.float32)), 0.0).astype(jnp.bfloat16)
    act_five = acts.reshape(BRICKS, BRICK, BRICK, BRICK, channels)
    grad_five = grad_pre.reshape(BRICKS, BRICK, BRICK, BRICK, channels)
    act_planes = (act_five[:, BRICK - 1:], act_five, act_five[:, :1])
    grad_planes = (grad_five[:, BRICK - 1:], grad_five, grad_five[:, :1])
    filt_flip = filt.reshape(27, channels, channels).transpose(0, 2, 1).reshape(27 * channels, channels)
    usable = neighbors < BRICKS
    indices = jnp.minimum(neighbors, BRICKS - 1).astype(jnp.int32)

    def per_device(running, operands):
        device_indices, device_usable = operands
        act_pad = assemble(act_planes, device_indices, device_usable)
        grad_pad = assemble(grad_planes, device_indices, device_usable)
        running, grads = run_bricks(act_pad, grad_pad, filt_flip, running)
        return (running, grads)
    start = jnp.zeros((27 * channels, channels), jnp.float32)
    filt_sum, grads = lax.scan(per_device, start, (indices.reshape(devices, SLOTS, 27), usable.reshape(devices, SLOTS, 27)))
    grads = grads.reshape(BRICKS, VOX, channels)
    input_grad = jnp.where(is_live[:, None, None], grads, 0.0).astype(jnp.bfloat16)
    return (input_grad, filt_sum * (1.0 / math.sqrt(BRICKS * VOX)))
```

```python
import math

import jax
import jax.numpy as jnp
from jax import lax
from jax.experimental import pallas as pl
from jax.experimental.pallas import tpu as pltpu
from jax.sharding import PartitionSpec as P


SLOTS = 12
VOX = 512
C = 128
DEVICES = 256
CHIPS = 128
BRICKS = SLOTS * DEVICES
F32 = jnp.float32
BF16 = jnp.bfloat16
MESH = pl.DeviceIdType.MESH
SEGMENTS = 3


def slope_times(cotangent, preact):
    values = preact.astype(F32)
    sigma = 1.0 / (1.0 + jnp.exp(-values))
    return cotangent.astype(F32) * (sigma * (1.0 + values * (1.0 - sigma)))


def kernel(
    counts, neighbors, acts_hbm, pre_hbm, cot_hbm, filt_ref, in_grad_hbm, filt_grad_ref,
    acts, pre, cot, grads, halo_out, halo_in, halo, pads, acts_t, weights, filt_sum, filt_full,
    own_rows, pair_rows, rows, rs_pair, rs_pair_in, sum1, send1, recv1, sum2, send2, recv2,
    send3, recv3, sum4, recv4, in_grad, load_sem, store_sem, halo_sems, pair_sems, gz_sems, g2_sems,
    g1_sems, gp_sems, rp_sems, r1_sems, r2_sems, r3_sems, r4_sems,
):
    chip = lax.axis_index("space")
    core = lax.axis_index("rep")
    device = chip * 2 + core
    z = chip % 8
    stride1 = 32 - 24 * core
    stride2 = 8 + 24 * core
    c1 = (chip // stride1) % 4
    c2 = (chip // stride2) % 4

    def to(chip_id, core_id):
        return {"space": chip_id, "rep": core_id}

    partner = to(chip, 1 - core)
    above = (device + 1) % DEVICES
    below = (device + DEVICES - 1) % DEVICES
    outer = (device + DEVICES - 1 + 2 * core) % DEVICES

    def peer1(t):
        return to(chip + ((c1 + t) % 4 - c1) * stride1, core)

    def peer2(t):
        return to(chip + ((c2 + t) % 4 - c2) * stride2, core)

    def peerz(t):
        return to(chip + (z + t) % 8 - z, core)

    def load(source, target, part, index):
        span = pl.ds(part * 4, 4)
        return pltpu.make_async_copy(source.at[span], target.at[span], load_sem.at[index * 3 + part])

    loads = [load(s, t, part, i) for i, (s, t) in enumerate(((pre_hbm, pre), (cot_hbm, cot), (acts_hbm, acts))) for part in range(3)]
    for item in loads:
        item.start()

    barrier = pltpu.get_barrier_semaphore()
    greeted = [partner, to(outer // 2, outer % 2)]
    greeted += [peerz(t) for t in range(1, 8)] + [peer1(t) for t in range(1, 4)] + [peer2(t) for t in range(1, 4)]
    for other in greeted:
        pl.semaphore_signal(barrier, inc=1, device_id=other, device_id_type=MESH)

    def remote(source, target, sems, index, other):
        return pltpu.make_async_remote_copy(
            src_ref=source, dst_ref=target, send_sem=sems.at[0, index], recv_sem=sems.at[1, index],
            device_id=other, device_id_type=MESH,
        )

    started = []

    def go(copies):
        for item in copies:
            item.start()
        started.extend(copies)
        return copies

    def arrive(copies):
        for item in copies:
            item.wait_recv()

    wide = jnp.concatenate([filt_ref[...].astype(F32), jnp.zeros((27, 64), F32)], axis=1)
    wide = jnp.where(core == 0, wide, pltpu.roll(wide, 64, 1))
    filt_sum[0:32, :] = jnp.zeros((32, C), F32)
    filt_sum[0:27, :] = wide
    own_rows[...] = filt_sum[0:32, :].astype(BF16)
    filt_sum[3456:3464, :] = jnp.zeros((8, C), F32)
    grads[SLOTS] = jnp.zeros((8, 8, 8, C), F32)
    halo[0, SLOTS] = jnp.zeros((1, 8, 8, C), F32)
    halo[1, SLOTS] = jnp.zeros((1, 8, 8, C), F32)

    for item in loads[:6]:
        item.wait()
    live_count = counts[device]

    def outer_layers(b, carry):
        for side, x in ((0, 0), (1, 7)):
            g = slope_times(cot[b, x * 64:(x + 1) * 64, :], pre[b, x * 64:(x + 1) * 64, :])
            g = jnp.where(b < live_count, g, 0.0)
            grads[b, x] = g.reshape(8, 8, C)
            halo_out[side, b] = g.astype(BF16)
        return carry

    lax.fori_loop(0, SLOTS, outer_layers, 0)
    pl.semaphore_wait(barrier, len(greeted))
    halos = go([
        remote(halo_out.at[0], halo_in.at[1], halo_sems, 0, to(below // 2, below % 2)),
        remote(halo_out.at[1], halo_in.at[0], halo_sems, 1, to(above // 2, above % 2)),
    ])
    gather_pair = go([remote(own_rows, pair_rows, pair_sems, 0, partner)])

    def inner_layers(b, carry):
        for x in range(1, 7):
            g = slope_times(cot[b, x * 64:(x + 1) * 64, :], pre[b, x * 64:(x + 1) * 64, :])
            grads[b, x] = jnp.where(b < live_count, g, 0.0).reshape(8, 8, C)
        return carry

    lax.fori_loop(0, SLOTS, inner_layers, 0)
    for item in loads[6:]:
        item.wait()

    arrive(gather_pair)
    chunk = own_rows[...].astype(F32) + pair_rows[...].astype(F32)
    rows[core, c1, c2, z] = jnp.where(core == 0, chunk[0:16], chunk[16:32]).astype(BF16)
    here = rows.at[core, c1, c2, z]
    gather_z = go([remote(here, here, gz_sems, t, peerz(t)) for t in range(1, 8)])

    def transpose_acts(b, carry):
        a = acts[b].astype(F32).reshape(32, 2, 8, C)
        span = pl.ds(pl.multiple_of(b * 256, 256), 256)
        for parity in range(2):
            acts_t[parity * C:(parity + 1) * C, span] = a[:, parity].reshape(256, C).T.astype(BF16)
        return carry

    lax.fori_loop(0, SLOTS, transpose_acts, 0)

    row = lax.broadcasted_iota(jnp.int32, (1, 8, C), 1)

    def assemble(b, source, layer, x_from, count, x_to):
        def slot(step_y, step_z):
            index = neighbors[b, layer * 9 + (step_y + 1) * 3 + step_z + 1]
            local = jnp.clip(index - (device + layer - 1) * SLOTS, 0, SLOTS - 1)
            return jnp.where((index < BRICKS) & (b < live_count), local, SLOTS)

        slots = {(sy, sz): slot(sy, sz) for sy in (-1, 0, 1) for sz in (-1, 0, 1)}
        for lane in range(2):
            tiles = []
            for pair in range(5):
                padded_y = 2 * pair + lane
                sy = -1 if padded_y == 0 else 1 if padded_y == 9 else 0
                y = (padded_y - 1) % 8
                mid, low, high = (source[slots[sy, sz], pl.ds(x_from, count), y] for sz in (0, -1, 1))
                tiles.append((
                    pltpu.roll(jnp.where(row == 7, low, mid), 1, 1),
                    mid,
                    pltpu.roll(jnp.where(row == 0, high, mid), 7, 1),
                ))
            for shift in range(3):
                for q in range(2):
                    for half in range(2):
                        both = jnp.concatenate([tiles[q + 2 * half][shift], tiles[q + 2 * half + 1][shift]], axis=1)
                        pads[shift, q, b, pl.ds(x_to, count), half * 16:(half + 1) * 16, lane * C:(lane + 1) * C] = both.astype(BF16)

    def assemble_own(i, carry):
        x = (i % 4) * 2
        assemble(i // 4, grads, 1, x, 2, x + 1)
        return carry

    lax.fori_loop(0, SLOTS * 4, assemble_own, 0)

    arrive(gather_z)
    here = rows.at[core, c1, c2]
    gather_2 = go([remote(here, here, g2_sems, t, peer2(t)) for t in range(1, 4)])

    def window(step_x, step_z, q, bricks):
        found = pads[2 - step_z, q, bricks, pl.ds(2 - step_x, 8), :, :]
        return found.reshape(found.shape[0] * 256, 256)

    def filter_terms(step_x, step_z, carry):
        left = acts_t[...]
        q0, q1 = (
            jnp.dot(left, window(step_x, step_z, q, pl.ds(0, SLOTS)), preferred_element_type=F32) for q in range(2)
        )
        for step_y, term in (
            (0, q1[:C, :C] + q1[C:, C:]),
            (1, q0[:C, C:] + q1[C:, :C]),
            (2, q0[:C, :C] + q0[C:, C:]),
        ):
            tap = step_x * 9 + step_y * 3 + step_z
            filt_sum[pl.ds(pl.multiple_of(tap * C, C), C), :] = term
        return carry

    lax.fori_loop(0, 3, lambda step_z, carry: filter_terms(1, step_z, carry), 0)

    arrive(gather_2)
    here = rows.at[core, c1]
    gather_1 = go([remote(here, here, g1_sems, t, peer1(t)) for t in range(1, 4)])

    arrive(halos)

    def widen(b, carry):
        for side in range(2):
            halo[side, b] = halo_in[side, b].astype(F32).reshape(1, 8, 8, C)
        return carry

    lax.fori_loop(0, SLOTS, widen, 0)

    def assemble_halo(b, carry):
        assemble(b, halo.at[0], 0, 0, 1, 0)
        assemble(b, halo.at[1], 2, 0, 1, 9)
        return carry

    lax.fori_loop(0, SLOTS, assemble_halo, 0)
    lax.fori_loop(0, 3, lambda step_z, carry: filter_terms(0, step_z, carry), 0)

    arrive(gather_1)
    here = rows.at[core]
    gather_last = go([remote(here, here, gp_sems, 0, partner)])

    lax.fori_loop(0, 3, lambda step_z, carry: filter_terms(2, step_z, carry), 0)

    def deal(i, carry):
        block = filt_sum.at[pl.ds(pl.multiple_of(i * 216, 8), 224)]
        for k in range(8):
            rs_pair[0, i // 4, i % 4, k] = block[27 * k:27 * k + 16]
            rs_pair[1, i % 4, i // 4, k] = block[27 * k + 16:27 * k + 32]
        return carry

    lax.fori_loop(0, 16, deal, 0)
    reduce_pair = go([remote(rs_pair.at[1 - core], rs_pair_in, rp_sems, 0, partner)])

    arrive(gather_last)

    def undeal(i, carry):
        block = filt_full.at[pl.ds(pl.multiple_of(i * 216, 8), 224)]
        for k in range(8):
            block[27 * k:27 * k + 16] = rows[0, i // 4, i % 4, k].astype(F32)
            block[27 * k + 16:27 * k + 32] = rows[1, i % 4, i // 4, k].astype(F32)
        return carry

    lax.fori_loop(0, 16, undeal, 0)

    def build_weights(i, carry):
        step_x, step_z = i // 3, i % 3
        taps = []
        for step_y in range(3):
            tap = step_x * 9 + step_y * 3 + step_z
            taps.append(filt_full[pl.ds(pl.multiple_of(tap * C, C), C), :].T.astype(BF16))
        zero = jnp.zeros((C, C), BF16)
        for q in range(2):
            for lane in range(2):
                for parity in range(2):
                    step_y = parity - (2 * q + lane - 1) + 1
                    block = taps[step_y] if 0 <= step_y <= 2 else zero
                    weights[i, q * 256 + lane * C:q * 256 + (lane + 1) * C, parity * C:(parity + 1) * C] = block
        return carry

    lax.fori_loop(0, 9, build_weights, 0)

    def input_terms(i, carry):
        total = None
        for step in range(9):
            for q in range(2):
                term = jnp.dot(
                    window(step // 3, step % 3, q, pl.ds(i * 2, 2)),
                    weights[step, q * 256:(q + 1) * 256, :],
                    preferred_element_type=F32,
                )
                total = term if total is None else total + term
        total = total.reshape(64, 8, 2 * C)
        both = jnp.stack([total[:, :, :C], total[:, :, C:]], axis=1)
        in_grad[pl.ds(i * 2, 2)] = both.reshape(2, VOX, C).astype(BF16)
        return carry

    stores = []

    def input_segment(part):
        lax.fori_loop(part * 2, part * 2 + 2, input_terms, 0)
        span = pl.ds(part * 4, 4)
        item = pltpu.make_async_copy(in_grad.at[span], in_grad_hbm.at[span], store_sem.at[part])
        item.start()
        stores.append(item)

    input_segment(0)

    arrive(reduce_pair)

    def add_pair(i, carry):
        total = rs_pair[core, i // 4, i % 4] + rs_pair_in[i // 4, i % 4]
        sum1[i // 4, i % 4] = total
        send1[i // 4, i % 4] = total.astype(BF16)
        return carry

    lax.fori_loop(0, 16, add_pair, 0)
    reduce_1 = go([remote(send1.at[(c1 + t) % 4], recv1.at[t - 1], r1_sems, t, peer1(t)) for t in range(1, 4)])

    input_segment(1)

    arrive(reduce_1)

    def add_1(i, carry):
        total = sum1[c1, i]
        for t in range(3):
            total = total + recv1[t, i].astype(F32)
        sum2[i] = total
        send2[i] = total.astype(BF16)
        return carry

    lax.fori_loop(0, 4, add_1, 0)
    reduce_2 = go([remote(send2.at[(c2 + t) % 4], recv2.at[t - 1], r2_sems, t, peer2(t)) for t in range(1, 4)])

    input_segment(2)

    arrive(reduce_2)
    total = sum2[c2]
    for t in range(3):
        total = total + recv2[t].astype(F32)
    sum2[0] = total
    send3[...] = total.astype(BF16)
    reduce_z = go([remote(send3.at[(z + t) % 8], recv3.at[t - 1], r3_sems, t, peerz(t)) for t in range(1, 8)])
    arrive(reduce_z)
    total = sum2[0, z]
    for t in range(7):
        total = total + recv3[t].astype(F32)
    sum4[...] = total
    reduce_last = go([remote(sum4, recv4, r4_sems, 0, partner)])
    arrive(reduce_last)
    scale = 1.0 / math.sqrt(BRICKS * VOX)
    mine, other = sum4[...], recv4[...]
    both = jnp.concatenate([jnp.where(core == 0, mine, other), jnp.where(core == 0, other, mine)], axis=0) * scale
    both = jnp.where(core == 0, both, pltpu.roll(both, 64, 1))
    filt_grad_ref[...] = both[0:27, 0:64]
    for item in stores:
        item.wait()
    for item in started:
        item.wait_send()


def on_device(acts, preact, cotangent, filt, counts, neighbors):
    vmem, dma = pltpu.VMEM, pltpu.SemaphoreType.DMA
    any_space = pl.BlockSpec(memory_space=pl.ANY)
    in_smem = pl.BlockSpec(memory_space=pltpu.SMEM)
    in_vmem = pl.BlockSpec(memory_space=pltpu.VMEM)
    return pl.pallas_call(
        kernel,
        out_shape=(
            jax.ShapeDtypeStruct((SLOTS, VOX, C), BF16),
            jax.ShapeDtypeStruct((27, 64), F32),
        ),
        in_specs=[in_smem, in_smem, any_space, any_space, any_space, in_vmem],
        out_specs=(any_space, in_vmem),
        scratch_shapes=[
            vmem((SLOTS, VOX, C), BF16),
            vmem((SLOTS, VOX, C), BF16),
            vmem((SLOTS, VOX, C), BF16),
            vmem((SLOTS + 1, 8, 8, 8, C), F32),
            vmem((2, SLOTS, 64, C), BF16),
            vmem((2, SLOTS, 64, C), BF16),
            vmem((2, SLOTS + 1, 1, 8, 8, C), F32),
            vmem((3, 2, SLOTS, 10, 32, 2 * C), BF16),
            vmem((2 * C, SLOTS * 256), BF16),
            vmem((9, 512, 256), BF16),
            vmem((3464, C), F32),
            vmem((3464, C), F32),
            vmem((32, C), BF16),
            vmem((32, C), BF16),
            vmem((2, 4, 4, 8, 16, C), BF16),
            vmem((2, 4, 4, 8, 16, C), F32),
            vmem((4, 4, 8, 16, C), F32),
            vmem((4, 4, 8, 16, C), F32),
            vmem((4, 4, 8, 16, C), BF16),
            vmem((3, 4, 8, 16, C), BF16),
            vmem((4, 8, 16, C), F32),
            vmem((4, 8, 16, C), BF16),
            vmem((3, 8, 16, C), BF16),
            vmem((8, 16, C), BF16),
            vmem((7, 16, C), BF16),
            vmem((16, C), F32),
            vmem((16, C), F32),
            vmem((SLOTS, VOX, C), BF16),
            dma((9,)), dma((SEGMENTS,)),
            dma((2, 2)), dma((2, 1)), dma((2, 8)), dma((2, 4)), dma((2, 4)), dma((2, 1)),
            dma((2, 1)), dma((2, 4)), dma((2, 4)), dma((2, 8)), dma((2, 1)),
        ],
        compiler_params=pltpu.CompilerParams(
            collective_id=0, has_side_effects=True, vmem_limit_bytes=62_000_000
        ),
        name="brick_backward",
    )(counts, neighbors, acts, preact, cotangent, filt)


def solution(mesh):
    in_specs = (
        P(("space", "rep"), None, None),
        P(("space", "rep"), None, None),
        P(("space", "rep"), None, None),
        P("space", "rep"),
        P(),
        P(("space", "rep"), None),
    )
    out_specs = (P(("space", "rep"), None, None), P("space", "rep"))
    return jax.shard_map(
        on_device, mesh=mesh, in_specs=in_specs, out_specs=out_specs, check_vma=False
    )
```

```python
import math

import jax
import jax.numpy as jnp
from jax import lax
from jax.experimental import pallas as pl
from jax.experimental.pallas import tpu as pltpu
from jax.sharding import PartitionSpec as P


SLOTS = 12
VOX = 512
C = 128
DEVICES = 256
CHIPS = 128
BRICKS = SLOTS * DEVICES
F32 = jnp.float32
BF16 = jnp.bfloat16
MESH = pl.DeviceIdType.MESH
ITEMS = 8


def slope_times(cotangent, preact):
    values = preact.astype(F32)
    sigma = 0.5 + 0.5 * jnp.tanh(0.5 * values)
    return cotangent.astype(F32) * (sigma * (1.0 + values * (1.0 - sigma)))


def kernel(
    counts, neighbors, neighbors_vmem, acts_hbm, pre_hbm, cot_hbm, filt_ref, in_grad_hbm, filt_grad_ref,
    acts, pre, cot, grads, own_g, other_g, halo_out, halo_in, table_in, table, pads, acts_t, weights,
    filt_sum, filt_full, rows, rs_pair, rs_pair_in, sum1, send1, recv1, send2, recv2, in_grad, returned,
    load_sem, store_sem, table_sem, pair_sems, halo_sems, gz_sems, gxy_sems, gp_sems, rp_sems, rxy_sems, rz_sems,
):
    chip = lax.axis_index("space")
    core = lax.axis_index("rep")
    device = chip * 2 + core
    z = chip % 8
    xy = chip // 8

    def to(chip_id, core_id):
        return {"space": chip_id, "rep": core_id}

    partner = to(chip, 1 - core)
    next_chip = (chip + 1) % CHIPS
    last_chip = (chip + CHIPS - 1) % CHIPS

    def peer_xy(t):
        return to((xy + t) % 16 * 8 + z, core)

    def peer_z(t):
        return to(xy * 8 + (z + t) % 8, core)

    def load(source, target, part, index):
        span = pl.ds(part * 4, 4)
        return pltpu.make_async_copy(source.at[span], target.at[span], load_sem.at[index * 3 + part])

    pairs = ((pre_hbm, pre), (cot_hbm, cot), (acts_hbm, acts))
    loads = [load(s, t, part, i) for i, (s, t) in enumerate(pairs) for part in range(3)]
    for item in loads:
        item.start()

    barrier = pltpu.get_barrier_semaphore()
    greeted = [partner, to(next_chip, 0), to(last_chip, 1)]
    greeted += [peer_z(t) for t in range(1, 8)] + [peer_xy(t) for t in range(1, 16)]
    for other in greeted:
        pl.semaphore_signal(barrier, inc=1, device_id=other, device_id_type=MESH)

    def remote(source, target, sems, index, other, landing=None):
        return pltpu.make_async_remote_copy(
            src_ref=source, dst_ref=target, send_sem=sems.at[0, index],
            recv_sem=sems.at[1, index if landing is None else landing],
            device_id=other, device_id_type=MESH,
        )

    started = []

    def go(copies):
        for item in copies:
            item.start()
        started.extend(copies)
        return copies

    def arrive(copies):
        for item in copies:
            item.wait_recv()

    left = lax.broadcasted_iota(jnp.int32, (1, C), 1) < 64

    def swap(top, bottom):
        return jnp.where(left, top, pltpu.roll(bottom, 64, 1)), jnp.where(left, pltpu.roll(top, 64, 1), bottom)

    filt_sum[0:32, :] = jnp.zeros((32, C), F32)
    filt_sum[0:27, 0:64] = filt_ref[...].astype(F32)
    rows[core, xy, z] = swap(filt_sum[0:16, :], filt_sum[16:32, :])[0].astype(BF16)
    filt_sum[3456:3464, :] = jnp.zeros((8, C), F32)
    empty = jnp.zeros((8, 8, C), F32)
    grads[0, SLOTS, 7] = empty
    grads[3, SLOTS, 0] = empty
    for x in range(8):
        grads[1, SLOTS, x] = empty
        grads[2, SLOTS, x] = empty

    own_count = counts[device]
    other_count = counts[device + 1 - 2 * core]
    for item in loads[:6]:
        item.wait()

    def outer_layer(b, carry):
        span = pl.ds(pl.multiple_of(core * 448, 64), 64)
        g = slope_times(cot[b, span, :], pre[b, span, :])
        grads[1 + core, b, 7 * core] = g.reshape(8, 8, C)
        halo_out[b] = g.astype(BF16)
        own_g[b, span, :] = g.astype(BF16)
        return carry

    lax.fori_loop(0, SLOTS, outer_layer, 0)
    pl.semaphore_wait(barrier, len(greeted))
    facing = (chip + CHIPS - 1 + 2 * core) % CHIPS
    go([remote(halo_out, halo_in.at[1 - core], halo_sems, side, to(facing, side), 1 - core) for side in range(2)])
    swap_table = go([remote(neighbors_vmem, table_in, pair_sems, 0, partner)])
    swap_acts = go([remote(acts_hbm.at[pl.ds(8, 4)], acts.at[pl.ds(SLOTS, 4)], pair_sems, 1, partner)])
    here = rows.at[core, xy, z]
    gather_z = go([remote(here, here, gz_sems, t, peer_z(t)) for t in range(1, 8)])

    def inner_layers(b, carry):
        for j in range(7):
            x = j + 1 - core
            span = pl.ds(pl.multiple_of(x * 64, 64), 64)
            g = slope_times(cot[b, span, :], pre[b, span, :])
            grads[1 + core, b, x] = g.reshape(8, 8, C)
            own_g[b, span, :] = g.astype(BF16)
        return carry

    lax.fori_loop(0, SLOTS, inner_layers, 0)
    swap_g = go([remote(own_g, other_g, pair_sems, 2, partner)])
    arrive(swap_table)
    table_copy = pltpu.make_async_copy(table_in, table, table_sem)
    table_copy.start()
    for item in loads[6:]:
        item.wait()
    arrive(swap_acts)

    def foreign(i):
        return (i >= 4) & (15 - i < other_count)

    def transpose_acts(i, carry):
        brick = jnp.where(foreign(i), SLOTS + 7 - i, i)
        a = acts[brick].astype(F32).reshape(32, 2, 8, C)
        span = pl.ds(pl.multiple_of(i * 256, 256), 256)
        for parity in range(2):
            acts_t[parity * C:(parity + 1) * C, span] = a[:, parity].reshape(256, C).T.astype(BF16)
        return carry

    lax.fori_loop(0, ITEMS, transpose_acts, 0)
    table_copy.wait()

    row = lax.broadcasted_iota(jnp.int32, (1, 8, C), 1)

    def assemble(i, layer, planes):
        taken = foreign(i)
        live = taken | (i < own_count)
        parity = jnp.where(taken, 1 - core, core)
        first = (chip * 2 + parity + layer - 1) * SLOTS
        mirror = jnp.where(i >= 4, 15 - i, i)

        def slot(step_y, step_z):
            tap = layer * 9 + (step_y + 1) * 3 + step_z + 1
            index = jnp.where(taken, table[mirror, tap], neighbors[i, tap])
            return jnp.where((index < BRICKS) & live, jnp.clip(index - first, 0, SLOTS - 1), SLOTS)

        slots = {(sy, sz): slot(sy, sz) for sy in (-1, 0, 1) for sz in (-1, 0, 1)}
        for x_from, count, x_to in planes:
            for lane in range(2):
                tiles = []
                for pair in range(5):
                    padded_y = 2 * pair + lane
                    sy = -1 if padded_y == 0 else 1 if padded_y == 9 else 0
                    y = (padded_y - 1) % 8
                    mid, low, high = (
                        grads[parity + layer, slots[sy, sz], x_from:x_from + count, y] for sz in (0, -1, 1)
                    )
                    tiles.append((
                        pltpu.roll(jnp.where(row == 7, low, mid), 1, 1),
                        mid,
                        pltpu.roll(jnp.where(row == 0, high, mid), 7, 1),
                    ))
                for shift in range(3):
                    for q in range(2):
                        for half in range(2):
                            both = jnp.concatenate(
                                [tiles[q + 2 * half][shift], tiles[q + 2 * half + 1][shift]], axis=1
                            )
                            pads[
                                shift, q, i, x_to:x_to + count, half * 16:(half + 1) * 16, lane * C:(lane + 1) * C
                            ] = both.astype(BF16)

    def assemble_own(i, carry):
        assemble(i, 1, [(x, 2, x + 1) for x in range(0, 8, 2)])
        return carry

    lax.fori_loop(0, 4, assemble_own, 0)
    arrive(gather_z)
    here = rows.at[core, xy]
    gather_xy = go([remote(here, here, gxy_sems, t, peer_xy(t)) for t in range(1, 16)])
    arrive(swap_g)

    def widen(b, carry):
        grads[2 - core, b] = other_g[b].astype(F32).reshape(8, 8, 8, C)
        return carry

    lax.fori_loop(0, SLOTS, widen, 0)
    lax.fori_loop(4, ITEMS, assemble_own, 0)

    def window(step_x, step_z, q, items):
        found = pads[2 - step_z, q, items, pl.ds(2 - step_x, 8), :, :]
        return found.reshape(found.shape[0] * 256, 256)

    def filter_terms(step_x, step_z, carry):
        lhs = acts_t[...]
        q0, q1 = (
            jnp.dot(lhs, window(step_x, step_z, q, pl.ds(0, ITEMS)), preferred_element_type=F32) for q in range(2)
        )
        for step_y, term in (
            (0, q1[:C, :C] + q1[C:, C:]),
            (1, q0[:C, C:] + q1[C:, :C]),
            (2, q0[:C, :C] + q0[C:, C:]),
        ):
            tap = step_x * 9 + step_y * 3 + step_z
            filt_sum[pl.ds(pl.multiple_of(tap * C, C), C), :] = term
        return carry

    lax.fori_loop(0, 3, lambda step_z, carry: filter_terms(1, step_z, carry), 0)

    for side in range(2):
        remote(halo_out, halo_in.at[side], halo_sems, 0, partner, side).wait_recv()

    def widen_halo(b, carry):
        grads[0, b, 7] = halo_in[0, b].astype(F32).reshape(8, 8, C)
        grads[3, b, 0] = halo_in[1, b].astype(F32).reshape(8, 8, C)
        return carry

    lax.fori_loop(0, SLOTS, widen_halo, 0)

    def assemble_halo(i, carry):
        assemble(i, 0, [(7, 1, 0)])
        assemble(i, 2, [(0, 1, 9)])
        return carry

    lax.fori_loop(0, ITEMS, assemble_halo, 0)
    lax.fori_loop(0, 3, lambda step_z, carry: filter_terms(0, step_z, carry), 0)

    def deal(i, carry):
        block = filt_sum.at[pl.ds(pl.multiple_of(i * 216, 8), 224)]
        for k in range(8):
            rs_pair[0, i, k], rs_pair[1, i, k] = swap(block[27 * k:27 * k + 16], block[27 * k + 16:27 * k + 32])
        return carry

    def pair_half(part):
        span = pl.ds(part * 8, 8)
        return go([remote(rs_pair.at[1 - core, span], rs_pair_in.at[span], rp_sems, part, partner)])

    def add_pair(i, carry):
        total = rs_pair[core, i] + rs_pair_in[i]
        sum1[i] = total
        send1[i] = total.astype(BF16)
        return carry

    def send_half(part):
        for target in range(part * 8, part * 8 + 8):
            @pl.when(target != xy)
            def _():
                remote(send1.at[target], recv1.at[xy], rxy_sems, target, to(target * 8 + z, core), xy).start()

    lax.fori_loop(0, 8, deal, 0)
    reduce_pair = pair_half(0)
    arrive(gather_xy)
    here = rows.at[core]
    gather_last = go([remote(here, here, gp_sems, 0, partner)])
    lax.fori_loop(0, 2, lambda step_z, carry: filter_terms(2, step_z, carry), 0)
    arrive(reduce_pair)
    lax.fori_loop(0, 8, add_pair, 0)
    send_half(0)
    lax.fori_loop(2, 3, lambda step_z, carry: filter_terms(2, step_z, carry), 0)
    lax.fori_loop(8, 16, deal, 0)
    reduce_pair = pair_half(1)

    arrive(gather_last)

    def undeal(i, carry):
        block = filt_full.at[pl.ds(pl.multiple_of(i * 216, 8), 224)]
        for k in range(8):
            top, bottom = swap(rows[0, i, k].astype(F32), rows[1, i, k].astype(F32))
            block[27 * k:27 * k + 16] = top
            block[27 * k + 16:27 * k + 32] = bottom
        return carry

    lax.fori_loop(0, 16, undeal, 0)
    arrive(reduce_pair)
    lax.fori_loop(8, 16, add_pair, 0)
    send_half(1)

    def build_weights(i, carry):
        step_x, step_z = i // 3, i % 3
        taps = []
        for step_y in range(3):
            tap = step_x * 9 + step_y * 3 + step_z
            taps.append(filt_full[pl.ds(pl.multiple_of(tap * C, C), C), :].T.astype(BF16))
        zero = jnp.zeros((C, C), BF16)
        for q in range(2):
            for lane in range(2):
                for parity in range(2):
                    step_y = parity - (2 * q + lane - 1) + 1
                    block = taps[step_y] if 0 <= step_y <= 2 else zero
                    weights[i, q * 256 + lane * C:q * 256 + (lane + 1) * C, parity * C:(parity + 1) * C] = block
        return carry

    lax.fori_loop(0, 9, build_weights, 0)

    def input_terms(pair):
        total = None
        for step in range(9):
            for q in range(2):
                term = jnp.dot(
                    window(step // 3, step % 3, q, pl.ds(pair * 2, 2)),
                    weights[step, q * 256:(q + 1) * 256, :],
                    preferred_element_type=F32,
                )
                total = term if total is None else total + term
        total = total.reshape(64, 8, 2 * C)
        both = jnp.stack([total[:, :, :C], total[:, :, C:]], axis=1)
        return both.reshape(2, VOX, C)

    stores = []

    def store(part):
        span = pl.ds(part * 4, 4)
        item = pltpu.make_async_copy(in_grad.at[span], in_grad_hbm.at[span], store_sem.at[part])
        item.start()
        stores.append(item)

    def upper_items(pair, carry):
        found = input_terms(pair)
        for k in range(2):
            i = pair * 2 + k
            taken = foreign(i)
            in_grad[i] = jnp.where(taken, 0.0, found[k]).astype(BF16)
            returned[7 - i] = jnp.where(taken, found[k], 0.0).astype(BF16)
        return carry

    lax.fori_loop(2, 4, upper_items, 0)
    give_back = go([remote(returned, in_grad.at[pl.ds(8, 4)], pair_sems, 3, partner)])
    store(1)

    def lower_items(pair, carry):
        in_grad[pl.ds(pair * 2, 2)] = input_terms(pair).astype(BF16)
        return carry

    lax.fori_loop(0, 2, lower_items, 0)
    store(0)
    arrive(give_back)
    store(2)

    for source in range(16):
        @pl.when(source != xy)
        def _():
            remote(send1.at[source], recv1.at[source], rxy_sems, source, partner).wait_recv()
    recv1[xy] = jnp.zeros((8, 16, C), BF16)
    total = sum1[xy]
    for t in range(16):
        total = total + recv1[t].astype(F32)
    sum1[xy] = total
    send2[...] = total.astype(BF16)
    reduce_z = go([remote(send2.at[(z + t) % 8], recv2.at[t - 1], rz_sems, t, peer_z(t)) for t in range(1, 8)])
    arrive(reduce_z)
    total = sum1[xy, z]
    for t in range(7):
        total = total + recv2[t].astype(F32)
    total = total * (1.0 / math.sqrt(BRICKS * VOX))
    filt_grad_ref[0:16, :] = total[:, 0:64]
    filt_grad_ref[16:27, :] = total[0:11, 64:128]
    for item in stores:
        item.wait()
    for item in started:
        item.wait_send()
    for target in range(16):
        @pl.when(target != xy)
        def _():
            remote(send1.at[target], recv1.at[target], rxy_sems, target, partner).wait_send()


def hand_over(source, filt_ref, target, filt_out, buffer, in_sem, out_sem):
    parts = [pl.ds(k * 4, 4) for k in range(3)]
    reads = [pltpu.make_async_copy(source.at[p], buffer.at[p], in_sem.at[k]) for k, p in enumerate(parts)]
    writes = [pltpu.make_async_copy(buffer.at[p], target.at[p], out_sem.at[k]) for k, p in enumerate(parts)]
    for item in reads:
        item.start()
    filt_out[...] = filt_ref[...]
    for k in range(3):
        reads[k].wait()
        writes[k].start()
    for item in writes:
        item.wait()


def on_device(acts, preact, cotangent, filt, counts, neighbors):
    vmem, dma = pltpu.VMEM, pltpu.SemaphoreType.DMA
    any_space = pl.BlockSpec(memory_space=pl.ANY)
    in_smem = pl.BlockSpec(memory_space=pltpu.SMEM)
    in_vmem = pl.BlockSpec(memory_space=pltpu.VMEM)
    out_shape = (
        jax.ShapeDtypeStruct((SLOTS, VOX, C), BF16),
        jax.ShapeDtypeStruct((27, 64), F32),
    )
    found = pl.pallas_call(
        kernel,
        out_shape=out_shape,
        in_specs=[in_smem, in_smem, in_vmem, any_space, any_space, any_space, in_vmem],
        out_specs=(any_space, in_vmem),
        scratch_shapes=[
            vmem((SLOTS + 4, VOX, C), BF16),
            vmem((SLOTS, VOX, C), BF16),
            vmem((SLOTS, VOX, C), BF16),
            vmem((4, SLOTS + 1, 8, 8, 8, C), F32),
            vmem((SLOTS, VOX, C), BF16),
            vmem((SLOTS, VOX, C), BF16),
            vmem((SLOTS, 64, C), BF16),
            vmem((2, SLOTS, 64, C), BF16),
            vmem((SLOTS, 27), jnp.int32),
            pltpu.SMEM((SLOTS, 27), jnp.int32),
            vmem((3, 2, ITEMS, 10, 32, 2 * C), BF16),
            vmem((2 * C, ITEMS * 256), BF16),
            vmem((9, 512, 256), BF16),
            vmem((3464, C), F32),
            vmem((3464, C), F32),
            vmem((2, 16, 8, 16, C), BF16),
            vmem((2, 16, 8, 16, C), F32),
            vmem((16, 8, 16, C), F32),
            vmem((16, 8, 16, C), F32),
            vmem((16, 8, 16, C), BF16),
            vmem((16, 8, 16, C), BF16),
            vmem((8, 16, C), BF16),
            vmem((7, 16, C), BF16),
            vmem((SLOTS, VOX, C), BF16),
            vmem((4, VOX, C), BF16),
            dma((9,)), dma((3,)), dma(()), dma((2, 4)), dma((2, 2)), dma((2, 8)), dma((2, 16)), dma((2, 1)),
            dma((2, 2)), dma((2, 16)), dma((2, 8)),
        ],
        compiler_params=pltpu.CompilerParams(
            collective_id=0, has_side_effects=True, vmem_limit_bytes=62_000_000
        ),
        name="brick_backward",
    )(counts, neighbors, neighbors, acts, preact, cotangent, filt)
    return pl.pallas_call(
        hand_over,
        out_shape=out_shape,
        in_specs=[any_space, in_vmem],
        out_specs=(any_space, in_vmem),
        scratch_shapes=[vmem((SLOTS, VOX, C), BF16), dma((3,)), dma((3,))],
        name="hand_over",
    )(*found)


def solution(mesh):
    in_specs = (
        P(("space", "rep"), None, None),
        P(("space", "rep"), None, None),
        P(("space", "rep"), None, None),
        P("space", "rep"),
        P(),
        P(("space", "rep"), None),
    )
    out_specs = (P(("space", "rep"), None, None), P("space", "rep"))
    return jax.shard_map(
        on_device, mesh=mesh, in_specs=in_specs, out_specs=out_specs, check_vma=False
    )
```

```python
import math

import jax
import jax.numpy as jnp
from jax import lax
from jax.experimental import pallas as pl
from jax.experimental.pallas import tpu as pltpu
from jax.sharding import PartitionSpec as P


SLOTS = 12
VOX = 512
C = 128
DEVICES = 256
CHIPS = 128
BRICKS = SLOTS * DEVICES
F32 = jnp.float32
BF16 = jnp.bfloat16
MESH = pl.DeviceIdType.MESH
ITEMS = 8


def slope_times(cotangent, preact):
    values = preact.astype(F32)
    sigma = 0.5 + 0.5 * jnp.tanh(0.5 * values)
    return cotangent.astype(F32) * (sigma * (1.0 + values * (1.0 - sigma)))


def kernel(
    counts, neighbors, acts_hbm, pre_hbm, cot_hbm, filt_ref, in_grad_hbm, filt_grad_ref,
    acts, pre, cot, grads, own_g, other_g, halo_out, halo_in, own_table, other_table, mixed_table, table, pads, acts_t, weights,
    filt_sum, filt_full, rows, rs_pair, rs_pair_in, sum1, send1, recv1, send2, recv2, in_grad, returned,
    load_sem, store_sem, table_sem, pair_sems, halo_sems, gz_sems, gxy_sems, gp_sems, rp_sems, rxy_sems, rz_sems,
):
    chip = lax.axis_index("space")
    core = lax.axis_index("rep")
    device = chip * 2 + core
    z = chip % 8
    xy = chip // 8

    def to(chip_id, core_id):
        return {"space": chip_id, "rep": core_id}

    partner = to(chip, 1 - core)
    next_chip = (chip + 1) % CHIPS
    last_chip = (chip + CHIPS - 1) % CHIPS

    def peer_xy(t):
        return to((xy + t) % 16 * 8 + z, core)

    def peer_z(t):
        return to(xy * 8 + (z + t) % 8, core)

    def load(source, target, part, index):
        span = pl.ds(part * 4, 4)
        return pltpu.make_async_copy(source.at[span], target.at[span], load_sem.at[index * 3 + part])

    pairs = ((pre_hbm, pre), (cot_hbm, cot), (acts_hbm, acts))
    loads = [load(s, t, part, i) for i, (s, t) in enumerate(pairs) for part in range(3)]
    for item in loads:
        item.start()

    barrier = pltpu.get_barrier_semaphore()
    greeted = [partner, to(next_chip, 0), to(last_chip, 1)]
    greeted += [peer_z(t) for t in range(1, 8)] + [peer_xy(t) for t in range(1, 16)]
    for other in greeted:
        pl.semaphore_signal(barrier, inc=1, device_id=other, device_id_type=MESH)

    def remote(source, target, sems, index, other, landing=None):
        return pltpu.make_async_remote_copy(
            src_ref=source, dst_ref=target, send_sem=sems.at[0, index],
            recv_sem=sems.at[1, index if landing is None else landing],
            device_id=other, device_id_type=MESH,
        )

    started = []

    def go(copies):
        for item in copies:
            item.start()
        started.extend(copies)
        return copies

    def arrive(copies):
        for item in copies:
            item.wait_recv()

    left = lax.broadcasted_iota(jnp.int32, (1, C), 1) < 64

    def swap(top, bottom):
        return jnp.where(left, top, pltpu.roll(bottom, 64, 1)), jnp.where(left, pltpu.roll(top, 64, 1), bottom)

    filt_sum[0:32, :] = jnp.zeros((32, C), F32)
    filt_sum[0:27, 0:64] = filt_ref[...].astype(F32)
    rows[core, xy, z] = swap(filt_sum[0:16, :], filt_sum[16:32, :])[0].astype(BF16)
    filt_sum[3456:3464, :] = jnp.zeros((8, C), F32)
    empty = jnp.zeros((8, 8, C), F32)
    grads[0, SLOTS, 7] = empty
    grads[3, SLOTS, 0] = empty
    for x in range(8):
        grads[1, SLOTS, x] = empty
        grads[2, SLOTS, x] = empty

    own_count = counts[device]
    other_count = counts[device + 1 - 2 * core]
    tap = lax.broadcasted_iota(jnp.int32, (SLOTS, 27), 1)
    brick = lax.broadcasted_iota(jnp.int32, (SLOTS, 27), 0)
    found = neighbors[...]
    first = (device - 1) * SLOTS + jnp.where(tap >= 9, SLOTS, 0) + jnp.where(tap >= 18, SLOTS, 0)
    own_table[...] = jnp.where(
        (found < BRICKS) & (brick < own_count), jnp.clip(found - first, 0, SLOTS - 1), SLOTS
    )
    for item in loads[:6]:
        item.wait()

    def outer_layer(b, carry):
        span = pl.ds(pl.multiple_of(core * 448, 64), 64)
        g = slope_times(cot[b, span, :], pre[b, span, :])
        grads[1 + core, b, 7 * core] = g.reshape(8, 8, C)
        halo_out[b] = g.astype(BF16)
        own_g[b, span, :] = g.astype(BF16)
        return carry

    lax.fori_loop(0, SLOTS, outer_layer, 0)
    pl.semaphore_wait(barrier, len(greeted))
    facing = (chip + CHIPS - 1 + 2 * core) % CHIPS
    go([remote(halo_out, halo_in.at[1 - core], halo_sems, side, to(facing, side), 1 - core) for side in range(2)])
    swap_table = go([remote(own_table, other_table, pair_sems, 0, partner)])
    swap_acts = go([remote(acts_hbm.at[pl.ds(8, 4)], acts.at[pl.ds(SLOTS, 4)], pair_sems, 1, partner)])
    here = rows.at[core, xy, z]
    gather_z = go([remote(here, here, gz_sems, t, peer_z(t)) for t in range(1, 8)])

    def inner_layers(b, carry):
        for j in range(7):
            x = j + 1 - core
            span = pl.ds(pl.multiple_of(x * 64, 64), 64)
            g = slope_times(cot[b, span, :], pre[b, span, :])
            grads[1 + core, b, x] = g.reshape(8, 8, C)
            own_g[b, span, :] = g.astype(BF16)
        return carry

    def foreign(i):
        return (i >= 4) & (15 - i < other_count)

    swap_g = []
    for part in range(3):
        lax.fori_loop(part * 4, part * 4 + 4, inner_layers, 0)
        span = pl.ds(part * 4, 4)
        swap_g += go([remote(own_g.at[span], other_g.at[span], pair_sems, 4 + part, partner)])
        if part == 0:
            arrive(swap_table)
            mixed_table[0:4, :] = own_table[0:4, :]
            for i in range(4, ITEMS):
                mixed_table[i:i + 1, :] = jnp.where(foreign(i), other_table[15 - i:16 - i, :], own_table[i:i + 1, :])
            table_copy = pltpu.make_async_copy(mixed_table, table, table_sem)
            table_copy.start()
    for item in loads[6:]:
        item.wait()
    arrive(gather_z)
    here = rows.at[core, xy]
    gather_xy = go([remote(here, here, gxy_sems, t, peer_xy(t)) for t in range(1, 16)])
    arrive(swap_acts)

    def transpose_acts(i, carry):
        brick = jnp.where(foreign(i), SLOTS + 7 - i, i)
        a = acts[brick].astype(F32).reshape(32, 2, 8, C)
        span = pl.ds(pl.multiple_of(i * 256, 256), 256)
        for parity in range(2):
            acts_t[parity * C:(parity + 1) * C, span] = a[:, parity].reshape(256, C).T.astype(BF16)
        return carry

    lax.fori_loop(0, ITEMS, transpose_acts, 0)
    table_copy.wait()

    row = lax.broadcasted_iota(jnp.int32, (1, 8, C), 1)

    def assemble(i, layer, planes):
        parity = jnp.where(foreign(i), 1 - core, core)
        slots = {(sy, sz): table[i, layer * 9 + (sy + 1) * 3 + sz + 1] for sy in (-1, 0, 1) for sz in (-1, 0, 1)}
        for x_from, count, x_to in planes:
            for lane in range(2):
                tiles = []
                for pair in range(5):
                    padded_y = 2 * pair + lane
                    sy = -1 if padded_y == 0 else 1 if padded_y == 9 else 0
                    y = (padded_y - 1) % 8
                    mid, low, high = (
                        grads[parity + layer, slots[sy, sz], x_from:x_from + count, y] for sz in (0, -1, 1)
                    )
                    tiles.append((
                        pltpu.roll(jnp.where(row == 7, low, mid), 1, 1),
                        mid,
                        pltpu.roll(jnp.where(row == 0, high, mid), 7, 1),
                    ))
                for shift in range(3):
                    for q in range(2):
                        for half in range(2):
                            both = jnp.concatenate(
                                [tiles[q + 2 * half][shift], tiles[q + 2 * half + 1][shift]], axis=1
                            )
                            pads[
                                shift, q, i, x_to:x_to + count, half * 16:(half + 1) * 16, lane * C:(lane + 1) * C
                            ] = both.astype(BF16)

    def assemble_own(i, carry):
        assemble(i, 1, [(x, 2, x + 1) for x in range(0, 8, 2)])
        return carry

    lax.fori_loop(0, 4, assemble_own, 0)
    arrive(swap_g)

    def widen(b, carry):
        grads[2 - core, b] = other_g[b].astype(F32).reshape(8, 8, 8, C)
        return carry

    lax.fori_loop(0, SLOTS, widen, 0)
    lax.fori_loop(4, ITEMS, assemble_own, 0)

    def window(step_x, step_z, q, items):
        found = pads[2 - step_z, q, items, pl.ds(2 - step_x, 8), :, :]
        return found.reshape(found.shape[0] * 256, 256)

    def filter_terms(step_x, step_z, carry):
        lhs = acts_t[...]
        q0, q1 = (
            jnp.dot(lhs, window(step_x, step_z, q, pl.ds(0, ITEMS)), preferred_element_type=F32) for q in range(2)
        )
        for step_y, term in (
            (0, q1[:C, :C] + q1[C:, C:]),
            (1, q0[:C, C:] + q1[C:, :C]),
            (2, q0[:C, :C] + q0[C:, C:]),
        ):
            tap = step_x * 9 + step_y * 3 + step_z
            filt_sum[pl.ds(pl.multiple_of(tap * C, C), C), :] = term
        return carry

    def deal(i, carry):
        block = filt_sum.at[pl.ds(pl.multiple_of(i * 216, 8), 224)]
        for k in range(8):
            rs_pair[0, i, k], rs_pair[1, i, k] = swap(block[27 * k:27 * k + 16], block[27 * k + 16:27 * k + 32])
        return carry

    parts = ((6, 10), (0, 6), (10, 16))

    def post_pair(part):
        low, high = parts[part]
        lax.fori_loop(low, high, deal, 0)
        span = pl.ds(low, high - low)
        return go([remote(rs_pair.at[1 - core, span], rs_pair_in.at[span], rp_sems, part, partner)])

    def add_pair(i, carry):
        total = rs_pair[core, i] + rs_pair_in[i]
        sum1[i] = total
        send1[i] = total.astype(BF16)
        return carry

    def send_on(part, reduce_pair):
        arrive(reduce_pair)
        low, high = parts[part]
        lax.fori_loop(low, high, add_pair, 0)
        for target in range(low, high):
            @pl.when(target != xy)
            def _():
                remote(send1.at[target], recv1.at[xy], rxy_sems, target, to(target * 8 + z, core), xy).start()

    lax.fori_loop(0, 3, lambda step_z, carry: filter_terms(1, step_z, carry), 0)
    reduce_pair = post_pair(0)

    for side in range(2):
        remote(halo_out, halo_in.at[side], halo_sems, 0, partner, side).wait_recv()

    def widen_halo(b, carry):
        grads[0, b, 7] = halo_in[0, b].astype(F32).reshape(8, 8, C)
        grads[3, b, 0] = halo_in[1, b].astype(F32).reshape(8, 8, C)
        return carry

    lax.fori_loop(0, SLOTS, widen_halo, 0)

    def assemble_halo(i, carry):
        assemble(i, 0, [(7, 1, 0)])
        assemble(i, 2, [(0, 1, 9)])
        return carry

    lax.fori_loop(0, ITEMS, assemble_halo, 0)
    send_on(0, reduce_pair)
    lax.fori_loop(0, 3, lambda step_z, carry: filter_terms(0, step_z, carry), 0)
    reduce_pair = post_pair(1)
    lax.fori_loop(0, 1, lambda step_z, carry: filter_terms(2, step_z, carry), 0)
    send_on(1, reduce_pair)
    lax.fori_loop(1, 3, lambda step_z, carry: filter_terms(2, step_z, carry), 0)
    reduce_pair = post_pair(2)
    arrive(gather_xy)
    here = rows.at[core]
    gather_last = go([remote(here, here, gp_sems, 0, partner)])
    send_on(2, reduce_pair)

    arrive(gather_last)

    def undeal(i, carry):
        block = filt_full.at[pl.ds(pl.multiple_of(i * 216, 8), 224)]
        for k in range(8):
            top, bottom = swap(rows[0, i, k].astype(F32), rows[1, i, k].astype(F32))
            block[27 * k:27 * k + 16] = top
            block[27 * k + 16:27 * k + 32] = bottom
        return carry

    lax.fori_loop(0, 16, undeal, 0)

    def build_weights(i, carry):
        step_x, step_z = i // 3, i % 3
        taps = []
        for step_y in range(3):
            tap = step_x * 9 + step_y * 3 + step_z
            taps.append(filt_full[pl.ds(pl.multiple_of(tap * C, C), C), :].T.astype(BF16))
        zero = jnp.zeros((C, C), BF16)
        for q in range(2):
            for lane in range(2):
                for parity in range(2):
                    step_y = parity - (2 * q + lane - 1) + 1
                    block = taps[step_y] if 0 <= step_y <= 2 else zero
                    weights[i, q * 256 + lane * C:q * 256 + (lane + 1) * C, parity * C:(parity + 1) * C] = block
        return carry

    lax.fori_loop(0, 9, build_weights, 0)

    def input_terms(pair):
        total = None
        for step in range(9):
            for q in range(2):
                term = jnp.dot(
                    window(step // 3, step % 3, q, pl.ds(pair * 2, 2)),
                    weights[step, q * 256:(q + 1) * 256, :],
                    preferred_element_type=F32,
                )
                total = term if total is None else total + term
        total = total.reshape(64, 8, 2 * C)
        both = jnp.stack([total[:, :, :C], total[:, :, C:]], axis=1)
        return both.reshape(2, VOX, C)

    stores = []

    def store(part):
        span = pl.ds(part * 4, 4)
        item = pltpu.make_async_copy(in_grad.at[span], in_grad_hbm.at[span], store_sem.at[part])
        item.start()
        stores.append(item)

    def upper_items(pair, carry):
        found = input_terms(pair)
        for k in range(2):
            i = pair * 2 + k
            taken = foreign(i)
            in_grad[i] = jnp.where(taken, 0.0, found[k]).astype(BF16)
            returned[7 - i] = jnp.where(taken, found[k], 0.0).astype(BF16)
        return carry

    lax.fori_loop(2, 4, upper_items, 0)
    give_back = go([remote(returned, in_grad.at[pl.ds(8, 4)], pair_sems, 3, partner)])
    store(1)

    def lower_items(pair, carry):
        in_grad[pl.ds(pair * 2, 2)] = input_terms(pair).astype(BF16)
        return carry

    lax.fori_loop(0, 2, lower_items, 0)
    store(0)
    arrive(give_back)
    store(2)

    for source in range(16):
        @pl.when(source != xy)
        def _():
            remote(send1.at[source], recv1.at[source], rxy_sems, source, partner).wait_recv()
    recv1[xy] = jnp.zeros((8, 16, C), BF16)
    total = sum1[xy]
    for t in range(16):
        total = total + recv1[t].astype(F32)
    sum1[xy] = total
    send2[...] = total.astype(BF16)
    reduce_z = go([remote(send2.at[(z + t) % 8], recv2.at[t - 1], rz_sems, t, peer_z(t)) for t in range(1, 8)])
    arrive(reduce_z)
    total = sum1[xy, z]
    for t in range(7):
        total = total + recv2[t].astype(F32)
    total = total * (1.0 / math.sqrt(BRICKS * VOX))
    filt_grad_ref[0:16, :] = total[:, 0:64]
    filt_grad_ref[16:27, :] = total[0:11, 64:128]
    for item in stores:
        item.wait()
    for item in started:
        item.wait_send()
    for target in range(16):
        @pl.when(target != xy)
        def _():
            remote(send1.at[target], recv1.at[target], rxy_sems, target, partner).wait_send()


def hand_over(source, filt_ref, target, filt_out, buffer, in_sem, out_sem):
    parts = [pl.ds(k * 4, 4) for k in range(3)]
    reads = [pltpu.make_async_copy(source.at[p], buffer.at[p], in_sem.at[k]) for k, p in enumerate(parts)]
    writes = [pltpu.make_async_copy(buffer.at[p], target.at[p], out_sem.at[k]) for k, p in enumerate(parts)]
    for item in reads:
        item.start()
    filt_out[...] = filt_ref[...]
    for k in range(3):
        reads[k].wait()
        writes[k].start()
    for item in writes:
        item.wait()


def on_device(acts, preact, cotangent, filt, counts, neighbors):
    vmem, dma = pltpu.VMEM, pltpu.SemaphoreType.DMA
    any_space = pl.BlockSpec(memory_space=pl.ANY)
    in_smem = pl.BlockSpec(memory_space=pltpu.SMEM)
    in_vmem = pl.BlockSpec(memory_space=pltpu.VMEM)
    out_shape = (
        jax.ShapeDtypeStruct((SLOTS, VOX, C), BF16),
        jax.ShapeDtypeStruct((27, 64), F32),
    )
    found = pl.pallas_call(
        kernel,
        out_shape=out_shape,
        in_specs=[in_smem, in_vmem, any_space, any_space, any_space, in_vmem],
        out_specs=(any_space, in_vmem),
        scratch_shapes=[
            vmem((SLOTS + 4, VOX, C), BF16),
            vmem((SLOTS, VOX, C), BF16),
            vmem((SLOTS, VOX, C), BF16),
            vmem((4, SLOTS + 1, 8, 8, 8, C), F32),
            vmem((SLOTS, VOX, C), BF16),
            vmem((SLOTS, VOX, C), BF16),
            vmem((SLOTS, 64, C), BF16),
            vmem((2, SLOTS, 64, C), BF16),
            vmem((SLOTS, 27), jnp.int32),
            vmem((SLOTS, 27), jnp.int32),
            vmem((ITEMS, 27), jnp.int32),
            pltpu.SMEM((ITEMS, 27), jnp.int32),
            vmem((3, 2, ITEMS, 10, 32, 2 * C), BF16),
            vmem((2 * C, ITEMS * 256), BF16),
            vmem((9, 512, 256), BF16),
            vmem((3464, C), F32),
            vmem((3464, C), F32),
            vmem((2, 16, 8, 16, C), BF16),
            vmem((2, 16, 8, 16, C), F32),
            vmem((16, 8, 16, C), F32),
            vmem((16, 8, 16, C), F32),
            vmem((16, 8, 16, C), BF16),
            vmem((16, 8, 16, C), BF16),
            vmem((8, 16, C), BF16),
            vmem((7, 16, C), BF16),
            vmem((SLOTS, VOX, C), BF16),
            vmem((4, VOX, C), BF16),
            dma((9,)), dma((3,)), dma(()), dma((2, 8)), dma((2, 2)), dma((2, 8)), dma((2, 16)), dma((2, 1)),
            dma((2, 3)), dma((2, 16)), dma((2, 8)),
        ],
        compiler_params=pltpu.CompilerParams(
            collective_id=0, has_side_effects=True, vmem_limit_bytes=62_000_000
        ),
        name="brick_backward",
    )(counts, neighbors, acts, preact, cotangent, filt)
    return pl.pallas_call(
        hand_over,
        out_shape=out_shape,
        in_specs=[any_space, in_vmem],
        out_specs=(any_space, in_vmem),
        scratch_shapes=[vmem((SLOTS, VOX, C), BF16), dma((3,)), dma((3,))],
        name="hand_over",
    )(*found)


def solution(mesh):
    in_specs = (
        P(("space", "rep"), None, None),
        P(("space", "rep"), None, None),
        P(("space", "rep"), None, None),
        P("space", "rep"),
        P(),
        P(("space", "rep"), None),
    )
    out_specs = (P(("space", "rep"), None, None), P("space", "rep"))
    return jax.shard_map(
        on_device, mesh=mesh, in_specs=in_specs, out_specs=out_specs, check_vma=False
    )
```

```python
import math

import jax
import jax.numpy as jnp
from jax import lax
from jax.experimental import pallas as pl
from jax.experimental.pallas import tpu as pltpu
from jax.sharding import PartitionSpec as P


SLOTS = 12
VOX = 512
C = 128
DEVICES = 256
CHIPS = 128
BRICKS = SLOTS * DEVICES
F32 = jnp.float32
BF16 = jnp.bfloat16
MESH = pl.DeviceIdType.MESH
ITEMS = 8


def slope_times(cotangent, preact):
    values = preact.astype(F32)
    sigma = 0.5 + 0.5 * jnp.tanh(0.5 * values)
    return cotangent.astype(F32) * (sigma * (1.0 + values * (1.0 - sigma)))


def kernel(
    counts, neighbors, acts_hbm, pre_hbm, cot_hbm, filt_ref, in_grad_hbm, filt_grad_ref,
    acts, pre, cot, grads, own_g, other_g, halo_out, halo_in, own_table, other_table, mixed_table, table, pads, acts_t, weights,
    filt_sum, filt_full, rows, rs_pair, rs_pair_in, sum1, send1, recv1, send2, recv2, in_grad, returned,
    load_sem, store_sem, table_sem, pair_sems, halo_sems, gz_sems, gxy_sems, gp_sems, rp_sems, rxy_sems, rz_sems,
):
    chip = lax.axis_index("space")
    core = lax.axis_index("rep")
    device = chip * 2 + core
    z = chip % 8
    xy = chip // 8

    def to(chip_id, core_id):
        return {"space": chip_id, "rep": core_id}

    partner = to(chip, 1 - core)
    next_chip = (chip + 1) % CHIPS
    last_chip = (chip + CHIPS - 1) % CHIPS

    def peer_xy(t):
        return to((xy + t) % 16 * 8 + z, core)

    def peer_z(t):
        return to(xy * 8 + (z + t) % 8, core)

    def load(source, target, part, index):
        span = pl.ds(part * 4, 4)
        return pltpu.make_async_copy(source.at[span], target.at[span], load_sem.at[index * 3 + part])

    pairs = ((pre_hbm, pre), (cot_hbm, cot), (acts_hbm, acts))
    loads = [load(s, t, part, i) for i, (s, t) in enumerate(pairs) for part in range(3)]
    for item in loads:
        item.start()

    barrier = pltpu.get_barrier_semaphore()
    greeted = [partner, to(next_chip, 0), to(last_chip, 1)]
    greeted += [peer_z(t) for t in range(1, 8)] + [peer_xy(t) for t in range(1, 16)]
    for other in greeted:
        pl.semaphore_signal(barrier, inc=1, device_id=other, device_id_type=MESH)

    def remote(source, target, sems, index, other, landing=None):
        return pltpu.make_async_remote_copy(
            src_ref=source, dst_ref=target, send_sem=sems.at[0, index],
            recv_sem=sems.at[1, index if landing is None else landing],
            device_id=other, device_id_type=MESH,
        )

    started = []

    def go(copies):
        for item in copies:
            item.start()
        started.extend(copies)
        return copies

    def arrive(copies):
        for item in copies:
            item.wait_recv()

    left = lax.broadcasted_iota(jnp.int32, (1, C), 1) < 64

    def swap(top, bottom):
        return jnp.where(left, top, pltpu.roll(bottom, 64, 1)), jnp.where(left, pltpu.roll(top, 64, 1), bottom)

    filt_sum[0:32, :] = jnp.zeros((32, C), F32)
    filt_sum[0:27, 0:64] = filt_ref[...].astype(F32)
    rows[core, xy, z] = swap(filt_sum[0:16, :], filt_sum[16:32, :])[0].astype(BF16)
    filt_sum[3456:3464, :] = jnp.zeros((8, C), F32)
    empty = jnp.zeros((8, 8, C), F32)
    grads[0, SLOTS, 7] = empty
    grads[3, SLOTS, 0] = empty
    for x in range(8):
        grads[1, SLOTS, x] = empty
        grads[2, SLOTS, x] = empty

    own_count = counts[device]
    other_count = counts[device + 1 - 2 * core]
    tap = lax.broadcasted_iota(jnp.int32, (SLOTS, 27), 1)
    brick = lax.broadcasted_iota(jnp.int32, (SLOTS, 27), 0)
    found = neighbors[...]
    first = (device - 1) * SLOTS + jnp.where(tap >= 9, SLOTS, 0) + jnp.where(tap >= 18, SLOTS, 0)
    own_table[...] = jnp.where(
        (found < BRICKS) & (brick < own_count), jnp.clip(found - first, 0, SLOTS - 1), SLOTS
    )
    for item in loads[:6]:
        item.wait()

    def outer_layer(b, carry):
        span = pl.ds(pl.multiple_of(core * 448, 64), 64)
        g = slope_times(cot[b, span, :], pre[b, span, :])
        grads[1 + core, b, 7 * core] = g.reshape(8, 8, C)
        halo_out[b] = g.astype(BF16)
        own_g[b, span, :] = g.astype(BF16)
        return carry

    lax.fori_loop(0, SLOTS, outer_layer, 0)
    pl.semaphore_wait(barrier, len(greeted))
    here = rows.at[core, xy, z]
    gather_z = go([remote(here, here, gz_sems, t, peer_z(t)) for t in range(1, 8)])
    facing = (chip + CHIPS - 1 + 2 * core) % CHIPS
    go([remote(halo_out, halo_in.at[1 - core], halo_sems, side, to(facing, side), 1 - core) for side in range(2)])
    swap_table = go([remote(own_table, other_table, pair_sems, 0, partner)])
    swap_acts = go([remote(acts_hbm.at[pl.ds(8, 4)], acts.at[pl.ds(SLOTS, 4)], pair_sems, 1, partner)])

    def inner_layers(b, carry):
        for j in range(7):
            x = j + 1 - core
            span = pl.ds(pl.multiple_of(x * 64, 64), 64)
            g = slope_times(cot[b, span, :], pre[b, span, :])
            grads[1 + core, b, x] = g.reshape(8, 8, C)
            own_g[b, span, :] = g.astype(BF16)
        return carry

    def foreign(i):
        return (i >= 4) & (15 - i < other_count)

    swap_g = []
    for part in range(3):
        lax.fori_loop(part * 4, part * 4 + 4, inner_layers, 0)
        span = pl.ds(part * 4, 4)
        swap_g += go([remote(own_g.at[span], other_g.at[span], pair_sems, 4 + part, partner)])
        if part == 0:
            arrive(swap_table)
            mixed_table[0:4, :] = own_table[0:4, :]
            for i in range(4, ITEMS):
                mixed_table[i:i + 1, :] = jnp.where(foreign(i), other_table[15 - i:16 - i, :], own_table[i:i + 1, :])
            table_copy = pltpu.make_async_copy(mixed_table, table, table_sem)
            table_copy.start()
    for item in loads[6:]:
        item.wait()
    arrive(swap_acts)

    def transpose_acts(i, carry):
        brick = jnp.where(foreign(i), SLOTS + 7 - i, i)
        a = acts[brick].astype(F32).reshape(32, 2, 8, C)
        span = pl.ds(pl.multiple_of(i * 256, 256), 256)
        for parity in range(2):
            acts_t[parity * C:(parity + 1) * C, span] = a[:, parity].reshape(256, C).T.astype(BF16)
        return carry

    lax.fori_loop(0, ITEMS, transpose_acts, 0)
    table_copy.wait()

    row = lax.broadcasted_iota(jnp.int32, (1, 8, C), 1)

    def assemble(i, layer, planes):
        parity = jnp.where(foreign(i), 1 - core, core)
        slots = {(sy, sz): table[i, layer * 9 + (sy + 1) * 3 + sz + 1] for sy in (-1, 0, 1) for sz in (-1, 0, 1)}
        for x_from, count, x_to in planes:
            for lane in range(2):
                tiles = []
                for pair in range(5):
                    padded_y = 2 * pair + lane
                    sy = -1 if padded_y == 0 else 1 if padded_y == 9 else 0
                    y = (padded_y - 1) % 8
                    mid, low, high = (
                        grads[parity + layer, slots[sy, sz], x_from:x_from + count, y] for sz in (0, -1, 1)
                    )
                    tiles.append((
                        pltpu.roll(jnp.where(row == 7, low, mid), 1, 1),
                        mid,
                        pltpu.roll(jnp.where(row == 0, high, mid), 7, 1),
                    ))
                for shift in range(3):
                    for q in range(2):
                        for half in range(2):
                            both = jnp.concatenate(
                                [tiles[q + 2 * half][shift], tiles[q + 2 * half + 1][shift]], axis=1
                            )
                            pads[
                                shift, q, i, x_to:x_to + count, half * 16:(half + 1) * 16, lane * C:(lane + 1) * C
                            ] = both.astype(BF16)

    def assemble_own(i, carry):
        assemble(i, 1, [(x, 2, x + 1) for x in range(0, 8, 2)])
        return carry

    lax.fori_loop(0, 4, assemble_own, 0)
    arrive(swap_g)

    def widen(b, carry):
        grads[2 - core, b] = other_g[b].astype(F32).reshape(8, 8, 8, C)
        return carry

    lax.fori_loop(0, SLOTS, widen, 0)
    lax.fori_loop(4, ITEMS, assemble_own, 0)

    def window(step_x, step_z, q, items):
        found = pads[2 - step_z, q, items, pl.ds(2 - step_x, 8), :, :]
        return found.reshape(found.shape[0] * 256, 256)

    def filter_terms(step_x, step_z, carry):
        lhs = acts_t[...]
        q0, q1 = (
            jnp.dot(lhs, window(step_x, step_z, q, pl.ds(0, ITEMS)), preferred_element_type=F32) for q in range(2)
        )
        for step_y, term in (
            (0, q1[:C, :C] + q1[C:, C:]),
            (1, q0[:C, C:] + q1[C:, :C]),
            (2, q0[:C, :C] + q0[C:, C:]),
        ):
            tap = step_x * 9 + step_y * 3 + step_z
            filt_sum[pl.ds(pl.multiple_of(tap * C, C), C), :] = term
        return carry

    def deal(i, carry):
        block = filt_sum.at[pl.ds(pl.multiple_of(i * 216, 8), 224)]
        for k in range(8):
            rs_pair[0, i, k], rs_pair[1, i, k] = swap(block[27 * k:27 * k + 16], block[27 * k + 16:27 * k + 32])
        return carry

    parts = ((6, 10), (0, 6), (10, 16))

    def post_pair(part):
        low, high = parts[part]
        lax.fori_loop(low, high, deal, 0)
        span = pl.ds(low, high - low)
        return go([remote(rs_pair.at[1 - core, span], rs_pair_in.at[span], rp_sems, part, partner)])

    def add_pair(i, carry):
        total = rs_pair[core, i] + rs_pair_in[i]
        sum1[i] = total
        send1[i] = total.astype(BF16)
        return carry

    def send_on(part, reduce_pair):
        arrive(reduce_pair)
        low, high = parts[part]
        lax.fori_loop(low, high, add_pair, 0)
        for target in range(low, high):
            @pl.when(target != xy)
            def _():
                remote(send1.at[target], recv1.at[xy], rxy_sems, target, to(target * 8 + z, core), xy).start()

    lax.fori_loop(0, 1, lambda step_z, carry: filter_terms(1, step_z, carry), 0)
    arrive(gather_z)
    here = rows.at[core, xy]
    gather_xy = go([remote(here, here, gxy_sems, t, peer_xy(t)) for t in range(1, 16)])
    lax.fori_loop(1, 3, lambda step_z, carry: filter_terms(1, step_z, carry), 0)
    reduce_pair = post_pair(0)

    for side in range(2):
        remote(halo_out, halo_in.at[side], halo_sems, 0, partner, side).wait_recv()

    def widen_halo(b, carry):
        grads[0, b, 7] = halo_in[0, b].astype(F32).reshape(8, 8, C)
        grads[3, b, 0] = halo_in[1, b].astype(F32).reshape(8, 8, C)
        return carry

    lax.fori_loop(0, SLOTS, widen_halo, 0)

    def assemble_halo(i, carry):
        assemble(i, 0, [(7, 1, 0)])
        assemble(i, 2, [(0, 1, 9)])
        return carry

    lax.fori_loop(0, ITEMS, assemble_halo, 0)
    send_on(0, reduce_pair)
    lax.fori_loop(0, 3, lambda step_z, carry: filter_terms(0, step_z, carry), 0)
    reduce_pair = post_pair(1)
    lax.fori_loop(0, 1, lambda step_z, carry: filter_terms(2, step_z, carry), 0)
    send_on(1, reduce_pair)
    lax.fori_loop(1, 3, lambda step_z, carry: filter_terms(2, step_z, carry), 0)
    reduce_pair = post_pair(2)
    arrive(gather_xy)
    here = rows.at[core]
    gather_last = go([remote(here, here, gp_sems, 0, partner)])
    send_on(2, reduce_pair)

    arrive(gather_last)

    def undeal(i, carry):
        block = filt_full.at[pl.ds(pl.multiple_of(i * 216, 8), 224)]
        for k in range(8):
            top, bottom = swap(rows[0, i, k].astype(F32), rows[1, i, k].astype(F32))
            block[27 * k:27 * k + 16] = top
            block[27 * k + 16:27 * k + 32] = bottom
        return carry

    lax.fori_loop(0, 16, undeal, 0)

    def build_weights(i, carry):
        step_x, step_z = i // 3, i % 3
        taps = []
        for step_y in range(3):
            tap = step_x * 9 + step_y * 3 + step_z
            taps.append(filt_full[pl.ds(pl.multiple_of(tap * C, C), C), :].T.astype(BF16))
        zero = jnp.zeros((C, C), BF16)
        for q in range(2):
            for lane in range(2):
                for parity in range(2):
                    step_y = parity - (2 * q + lane - 1) + 1
                    block = taps[step_y] if 0 <= step_y <= 2 else zero
                    weights[i, q * 256 + lane * C:q * 256 + (lane + 1) * C, parity * C:(parity + 1) * C] = block
        return carry

    lax.fori_loop(0, 9, build_weights, 0)

    def input_terms(pair):
        total = None
        for step in range(9):
            for q in range(2):
                term = jnp.dot(
                    window(step // 3, step % 3, q, pl.ds(pair * 2, 2)),
                    weights[step, q * 256:(q + 1) * 256, :],
                    preferred_element_type=F32,
                )
                total = term if total is None else total + term
        total = total.reshape(64, 8, 2 * C)
        both = jnp.stack([total[:, :, :C], total[:, :, C:]], axis=1)
        return both.reshape(2, VOX, C)

    stores = []

    def store(part):
        span = pl.ds(part * 4, 4)
        item = pltpu.make_async_copy(in_grad.at[span], in_grad_hbm.at[span], store_sem.at[part])
        item.start()
        stores.append(item)

    def upper_items(pair, carry):
        found = input_terms(pair)
        for k in range(2):
            i = pair * 2 + k
            taken = foreign(i)
            in_grad[i] = jnp.where(taken, 0.0, found[k]).astype(BF16)
            returned[7 - i] = jnp.where(taken, found[k], 0.0).astype(BF16)
        return carry

    lax.fori_loop(2, 4, upper_items, 0)
    give_back = go([remote(returned, in_grad.at[pl.ds(8, 4)], pair_sems, 3, partner)])
    store(1)

    for source in range(16):
        @pl.when(source != xy)
        def _():
            remote(send1.at[source], recv1.at[source], rxy_sems, source, partner).wait_recv()
    recv1[xy] = jnp.zeros((8, 16, C), BF16)
    total = sum1[xy]
    for t in range(16):
        total = total + recv1[t].astype(F32)
    sum1[xy] = total
    send2[...] = total.astype(BF16)
    reduce_z = go([remote(send2.at[(z + t) % 8], recv2.at[t - 1], rz_sems, t, peer_z(t)) for t in range(1, 8)])

    def lower_items(pair, carry):
        in_grad[pl.ds(pair * 2, 2)] = input_terms(pair).astype(BF16)
        return carry

    lax.fori_loop(0, 2, lower_items, 0)
    store(0)
    arrive(give_back)
    store(2)

    arrive(reduce_z)
    total = sum1[xy, z]
    for t in range(7):
        total = total + recv2[t].astype(F32)
    total = total * (1.0 / math.sqrt(BRICKS * VOX))
    filt_grad_ref[0:16, :] = total[:, 0:64]
    filt_grad_ref[16:27, :] = total[0:11, 64:128]
    for item in stores:
        item.wait()
    for item in started:
        item.wait_send()
    for target in range(16):
        @pl.when(target != xy)
        def _():
            remote(send1.at[target], recv1.at[target], rxy_sems, target, partner).wait_send()


def hand_over(source, filt_ref, target, filt_out, buffer, in_sem, out_sem):
    parts = [pl.ds(k * 4, 4) for k in range(3)]
    reads = [pltpu.make_async_copy(source.at[p], buffer.at[p], in_sem.at[k]) for k, p in enumerate(parts)]
    writes = [pltpu.make_async_copy(buffer.at[p], target.at[p], out_sem.at[k]) for k, p in enumerate(parts)]
    for item in reads:
        item.start()
    filt_out[...] = filt_ref[...]
    for k in range(3):
        reads[k].wait()
        writes[k].start()
    for item in writes:
        item.wait()


def on_device(acts, preact, cotangent, filt, counts, neighbors):
    vmem, dma = pltpu.VMEM, pltpu.SemaphoreType.DMA
    any_space = pl.BlockSpec(memory_space=pl.ANY)
    in_smem = pl.BlockSpec(memory_space=pltpu.SMEM)
    in_vmem = pl.BlockSpec(memory_space=pltpu.VMEM)
    out_shape = (
        jax.ShapeDtypeStruct((SLOTS, VOX, C), BF16),
        jax.ShapeDtypeStruct((27, 64), F32),
    )
    found = pl.pallas_call(
        kernel,
        out_shape=out_shape,
        in_specs=[in_smem, in_vmem, any_space, any_space, any_space, in_vmem],
        out_specs=(any_space, in_vmem),
        scratch_shapes=[
            vmem((SLOTS + 4, VOX, C), BF16),
            vmem((SLOTS, VOX, C), BF16),
            vmem((SLOTS, VOX, C), BF16),
            vmem((4, SLOTS + 1, 8, 8, 8, C), F32),
            vmem((SLOTS, VOX, C), BF16),
            vmem((SLOTS, VOX, C), BF16),
            vmem((SLOTS, 64, C), BF16),
            vmem((2, SLOTS, 64, C), BF16),
            vmem((SLOTS, 27), jnp.int32),
            vmem((SLOTS, 27), jnp.int32),
            vmem((ITEMS, 27), jnp.int32),
            pltpu.SMEM((ITEMS, 27), jnp.int32),
            vmem((3, 2, ITEMS, 10, 32, 2 * C), BF16),
            vmem((2 * C, ITEMS * 256), BF16),
            vmem((9, 512, 256), BF16),
            vmem((3464, C), F32),
            vmem((3464, C), F32),
            vmem((2, 16, 8, 16, C), BF16),
            vmem((2, 16, 8, 16, C), F32),
            vmem((16, 8, 16, C), F32),
            vmem((16, 8, 16, C), F32),
            vmem((16, 8, 16, C), BF16),
            vmem((16, 8, 16, C), BF16),
            vmem((8, 16, C), BF16),
            vmem((7, 16, C), BF16),
            vmem((SLOTS, VOX, C), BF16),
            vmem((4, VOX, C), BF16),
            dma((9,)), dma((3,)), dma(()), dma((2, 8)), dma((2, 2)), dma((2, 8)), dma((2, 16)), dma((2, 1)),
            dma((2, 3)), dma((2, 16)), dma((2, 8)),
        ],
        compiler_params=pltpu.CompilerParams(
            collective_id=0, has_side_effects=True, vmem_limit_bytes=62_000_000
        ),
        name="brick_backward",
    )(counts, neighbors, acts, preact, cotangent, filt)
    return pl.pallas_call(
        hand_over,
        out_shape=out_shape,
        in_specs=[any_space, in_vmem],
        out_specs=(any_space, in_vmem),
        scratch_shapes=[vmem((SLOTS, VOX, C), BF16), dma((3,)), dma((3,))],
        name="hand_over",
    )(*found)


def solution(mesh):
    in_specs = (
        P(("space", "rep"), None, None),
        P(("space", "rep"), None, None),
        P(("space", "rep"), None, None),
        P("space", "rep"),
        P(),
        P(("space", "rep"), None),
    )
    out_specs = (P(("space", "rep"), None, None), P("space", "rep"))
    return jax.shard_map(
        on_device, mesh=mesh, in_specs=in_specs, out_specs=out_specs, check_vma=False
    )
```

```python
import math

import jax
import jax.numpy as jnp
from jax import lax
from jax.experimental import pallas as pl
from jax.experimental.pallas import tpu as pltpu
from jax.sharding import PartitionSpec as P


SLOTS = 12
VOX = 512
C = 128
DEVICES = 256
CHIPS = 128
BRICKS = SLOTS * DEVICES
F32 = jnp.float32
BF16 = jnp.bfloat16
MESH = pl.DeviceIdType.MESH
ITEMS = 8


def slope_times(cotangent, preact):
    values = preact.astype(F32)
    sigma = 0.5 + 0.5 * jnp.tanh(0.5 * values)
    return cotangent.astype(F32) * (sigma * (1.0 + values * (1.0 - sigma)))


def kernel(
    counts, neighbors, acts_hbm, pre_hbm, cot_hbm, filt_ref, in_grad, filt_grad_ref,
    acts, pre, cot, grads, own_g, other_g, halo_out, halo_in, own_table, other_table, mixed_table, table, pads, acts_t, weights,
    filt_sum, filt_full, rows, rs_pair, rs_pair_in, sum1, send1, recv1, send2, recv2, returned, landed,
    load_sem, store_sem, table_sem, pair_sems, halo_sems, gz_sems, gxy_sems, gp_sems, rp_sems, rxy_sems, rz_sems,
):
    chip = lax.axis_index("space")
    core = lax.axis_index("rep")
    device = chip * 2 + core
    z = chip % 8
    xy = chip // 8

    def to(chip_id, core_id):
        return {"space": chip_id, "rep": core_id}

    partner = to(chip, 1 - core)

    def peer_xy(t):
        return to((xy + t) % 16 * 8 + z, core)

    def peer_z(t):
        return to(xy * 8 + (z + t) % 8, core)

    def load(source, target, part, index):
        span = pl.ds(part * 4, 4)
        return pltpu.make_async_copy(source.at[span], target.at[span], load_sem.at[index * 3 + part])

    pairs = ((pre_hbm, pre), (cot_hbm, cot), (acts_hbm, acts))
    loads = [load(s, t, part, i) for i, (s, t) in enumerate(pairs) for part in range(3)]
    for item in loads[:6]:
        item.start()

    barrier = pltpu.get_barrier_semaphore()
    facing = to((chip + CHIPS - 1 + 2 * core) % CHIPS, 1 - core)
    greeted = [partner, facing]
    greeted += [peer_z(t) for t in range(1, 8)] + [peer_xy(t) for t in range(1, 16)]
    for other in greeted:
        pl.semaphore_signal(barrier, inc=1, device_id=other, device_id_type=MESH)

    def remote(source, target, sems, index, other, landing=None):
        return pltpu.make_async_remote_copy(
            src_ref=source, dst_ref=target, send_sem=sems.at[0, index],
            recv_sem=sems.at[1, index if landing is None else landing],
            device_id=other, device_id_type=MESH,
        )

    started = []

    def go(copies):
        for item in copies:
            item.start()
        started.extend(copies)
        return copies

    def arrive(copies):
        for item in copies:
            item.wait_recv()

    left = lax.broadcasted_iota(jnp.int32, (1, C), 1) < 64

    def swap(top, bottom):
        return jnp.where(left, top, pltpu.roll(bottom, 64, 1)), jnp.where(left, pltpu.roll(top, 64, 1), bottom)

    filt_sum[0:32, :] = jnp.zeros((32, C), F32)
    filt_sum[0:27, 0:64] = filt_ref[...].astype(F32)
    rows[core, xy, z] = swap(filt_sum[0:16, :], filt_sum[16:32, :])[0].astype(BF16)
    filt_sum[3456:3464, :] = jnp.zeros((8, C), F32)
    empty = jnp.zeros((8, 8, C), F32)
    grads[0, SLOTS, 7] = empty
    grads[3, SLOTS, 0] = empty
    for x in range(8):
        grads[1, SLOTS, x] = empty
        grads[2, SLOTS, x] = empty

    own_count = counts[device]
    other_count = counts[device + 1 - 2 * core]
    tap = lax.broadcasted_iota(jnp.int32, (SLOTS, 27), 1)
    brick = lax.broadcasted_iota(jnp.int32, (SLOTS, 27), 0)
    found = neighbors[...]
    first = (device - 1) * SLOTS + jnp.where(tap >= 9, SLOTS, 0) + jnp.where(tap >= 18, SLOTS, 0)
    own_table[...] = jnp.where(
        (found < BRICKS) & (brick < own_count), jnp.clip(found - first, 0, SLOTS - 1), SLOTS
    )
    for item in loads[:6]:
        item.wait()
    for item in loads[6:]:
        item.start()

    def outer_layer(b, carry):
        span = pl.ds(pl.multiple_of(core * 448, 64), 64)
        g = slope_times(cot[b, span, :], pre[b, span, :])
        grads[1 + core, b, 7 * core] = g.reshape(8, 8, C)
        halo_out[b] = g.astype(BF16)
        own_g[b, span, :] = g.astype(BF16)
        return carry

    lax.fori_loop(0, SLOTS, outer_layer, 0)
    pl.semaphore_wait(barrier, len(greeted))
    here = rows.at[core, xy, z]
    gather_z = go([remote(here, here, gz_sems, t, peer_z(t)) for t in range(1, 8)])
    go([remote(halo_out, halo_in.at[1 - core], halo_sems, 0, facing, 1 - core)])
    swap_table = go([remote(own_table, other_table, pair_sems, 0, partner)])

    def inner_layers(b, carry):
        for j in range(7):
            x = j + 1 - core
            span = pl.ds(pl.multiple_of(x * 64, 64), 64)
            g = slope_times(cot[b, span, :], pre[b, span, :])
            grads[1 + core, b, x] = g.reshape(8, 8, C)
            own_g[b, span, :] = g.astype(BF16)
        return carry

    def foreign(i):
        return (i >= 4) & (15 - i < other_count)

    swap_g = []
    for part in range(3):
        lax.fori_loop(part * 4, part * 4 + 4, inner_layers, 0)
        span = pl.ds(part * 4, 4)
        swap_g += go([remote(own_g.at[span], other_g.at[span], pair_sems, 4 + part, partner)])
        if part == 0:
            arrive(swap_table)
            mixed_table[0:4, :] = own_table[0:4, :]
            for i in range(4, ITEMS):
                mixed_table[i:i + 1, :] = jnp.where(foreign(i), other_table[15 - i:16 - i, :], own_table[i:i + 1, :])
            table_copy = pltpu.make_async_copy(mixed_table, table, table_sem)
            table_copy.start()
    swap_acts = go([remote(acts_hbm.at[pl.ds(8, 4)], acts.at[pl.ds(SLOTS, 4)], pair_sems, 1, partner)])
    for item in loads[6:]:
        item.wait()

    def transpose_acts(i, brick):
        a = acts[brick].astype(F32).reshape(32, 2, 8, C)
        span = pl.ds(pl.multiple_of(i * 256, 256), 256)
        for parity in range(2):
            acts_t[parity * C:(parity + 1) * C, span] = a[:, parity].reshape(256, C).T.astype(BF16)

    def lower_acts(i, carry):
        transpose_acts(i, i)
        return carry

    def upper_acts(i, carry):
        transpose_acts(i, jnp.where(foreign(i), SLOTS + 7 - i, i))
        return carry

    lax.fori_loop(0, 4, lower_acts, 0)
    table_copy.wait()

    row = lax.broadcasted_iota(jnp.int32, (1, 8, C), 1)

    def assemble(i, layer, planes):
        parity = jnp.where(foreign(i), 1 - core, core)
        slots = {(sy, sz): table[i, layer * 9 + (sy + 1) * 3 + sz + 1] for sy in (-1, 0, 1) for sz in (-1, 0, 1)}
        for x_from, count, x_to in planes:
            for lane in range(2):
                tiles = []
                for pair in range(5):
                    padded_y = 2 * pair + lane
                    sy = -1 if padded_y == 0 else 1 if padded_y == 9 else 0
                    y = (padded_y - 1) % 8
                    mid, low, high = (
                        grads[parity + layer, slots[sy, sz], x_from:x_from + count, y] for sz in (0, -1, 1)
                    )
                    tiles.append((
                        pltpu.roll(jnp.where(row == 7, low, mid), 1, 1),
                        mid,
                        pltpu.roll(jnp.where(row == 0, high, mid), 7, 1),
                    ))
                for shift in range(3):
                    for q in range(2):
                        for half in range(2):
                            both = jnp.concatenate(
                                [tiles[q + 2 * half][shift], tiles[q + 2 * half + 1][shift]], axis=1
                            )
                            pads[
                                shift, q, i, x_to:x_to + count, half * 16:(half + 1) * 16, lane * C:(lane + 1) * C
                            ] = both.astype(BF16)

    def assemble_own(i, carry):
        assemble(i, 1, [(x, 2, x + 1) for x in range(0, 8, 2)])
        return carry

    lax.fori_loop(0, 4, assemble_own, 0)
    arrive(swap_g[:2])

    def widen(b, carry):
        grads[2 - core, b] = other_g[b].astype(F32).reshape(8, 8, 8, C)
        return carry

    lax.fori_loop(0, 8, widen, 0)
    arrive(swap_g[2:])
    lax.fori_loop(8, SLOTS, widen, 0)
    lax.fori_loop(4, ITEMS, assemble_own, 0)
    arrive(gather_z)
    here = rows.at[core, xy]
    gather_xy = go([remote(here, here, gxy_sems, t, peer_xy(t)) for t in range(1, 16)])
    arrive(swap_acts)
    lax.fori_loop(4, ITEMS, upper_acts, 0)

    def window(step_x, step_z, q, items):
        found = pads[2 - step_z, q, items, pl.ds(2 - step_x, 8), :, :]
        return found.reshape(found.shape[0] * 256, 256)

    def filter_terms(step_x, step_z, carry):
        lhs = acts_t[...]
        q0, q1 = (
            jnp.dot(lhs, window(step_x, step_z, q, pl.ds(0, ITEMS)), preferred_element_type=F32) for q in range(2)
        )
        for step_y, term in (
            (0, q1[:C, :C] + q1[C:, C:]),
            (1, q0[:C, C:] + q1[C:, :C]),
            (2, q0[:C, :C] + q0[C:, C:]),
        ):
            tap = step_x * 9 + step_y * 3 + step_z
            filt_sum[pl.ds(pl.multiple_of(tap * C, C), C), :] = term
        return carry

    def deal(i, carry):
        block = filt_sum.at[pl.ds(pl.multiple_of(i * 216, 8), 224)]
        for k in range(8):
            rs_pair[0, i, k], rs_pair[1, i, k] = swap(block[27 * k:27 * k + 16], block[27 * k + 16:27 * k + 32])
        return carry

    parts = ((6, 10), (0, 6), (10, 16))

    def post_pair(part):
        low, high = parts[part]
        lax.fori_loop(low, high, deal, 0)
        span = pl.ds(low, high - low)
        return go([remote(rs_pair.at[1 - core, span], rs_pair_in.at[span], rp_sems, part, partner)])

    def add_pair(i, carry):
        total = rs_pair[core, i] + rs_pair_in[i]
        sum1[i] = total
        send1[i] = total.astype(BF16)
        return carry

    def send_on(part, reduce_pair):
        arrive(reduce_pair)
        low, high = parts[part]
        lax.fori_loop(low, high, add_pair, 0)
        for target in range(low, high):
            @pl.when(target != xy)
            def _():
                remote(send1.at[target], recv1.at[xy], rxy_sems, target, to(target * 8 + z, core), xy).start()

    lax.fori_loop(0, 1, lambda step_z, carry: filter_terms(1, step_z, carry), 0)
    remote(halo_out, halo_in.at[core], halo_sems, 0, partner, core).wait_recv()
    go([remote(halo_in.at[core], halo_in.at[core], halo_sems, 1, partner, core)])
    lax.fori_loop(1, 3, lambda step_z, carry: filter_terms(1, step_z, carry), 0)
    reduce_pair = post_pair(0)

    remote(halo_out, halo_in.at[1 - core], halo_sems, 0, partner, 1 - core).wait_recv()

    def widen_halo(b, carry):
        grads[0, b, 7] = halo_in[0, b].astype(F32).reshape(8, 8, C)
        grads[3, b, 0] = halo_in[1, b].astype(F32).reshape(8, 8, C)
        return carry

    lax.fori_loop(0, SLOTS, widen_halo, 0)

    def assemble_halo(i, carry):
        assemble(i, 0, [(7, 1, 0)])
        assemble(i, 2, [(0, 1, 9)])
        return carry

    lax.fori_loop(0, ITEMS, assemble_halo, 0)
    lax.fori_loop(0, 1, lambda step_z, carry: filter_terms(0, step_z, carry), 0)
    send_on(0, reduce_pair)
    lax.fori_loop(1, 3, lambda step_z, carry: filter_terms(0, step_z, carry), 0)
    reduce_pair = post_pair(1)
    lax.fori_loop(0, 2, lambda step_z, carry: filter_terms(2, step_z, carry), 0)
    send_on(1, reduce_pair)
    lax.fori_loop(2, 3, lambda step_z, carry: filter_terms(2, step_z, carry), 0)
    reduce_pair = post_pair(2)
    send_on(2, reduce_pair)
    arrive(gather_xy)
    here = rows.at[core]
    gather_last = go([remote(here, here, gp_sems, 0, partner)])

    arrive(gather_last)

    def undeal(i, carry):
        block = filt_full.at[pl.ds(pl.multiple_of(i * 216, 8), 224)]
        for k in range(8):
            top, bottom = swap(rows[0, i, k].astype(F32), rows[1, i, k].astype(F32))
            block[27 * k:27 * k + 16] = top
            block[27 * k + 16:27 * k + 32] = bottom
        return carry

    lax.fori_loop(0, 16, undeal, 0)

    def build_weights(i, carry):
        step_x, step_z = i // 3, i % 3
        taps = []
        for step_y in range(3):
            tap = step_x * 9 + step_y * 3 + step_z
            taps.append(filt_full[pl.ds(pl.multiple_of(tap * C, C), C), :].T.astype(BF16))
        zero = jnp.zeros((C, C), BF16)
        for q in range(2):
            for lane in range(2):
                for parity in range(2):
                    step_y = parity - (2 * q + lane - 1) + 1
                    block = taps[step_y] if 0 <= step_y <= 2 else zero
                    weights[i, q * 256 + lane * C:q * 256 + (lane + 1) * C, parity * C:(parity + 1) * C] = block
        return carry

    lax.fori_loop(0, 9, build_weights, 0)

    def input_terms(pair):
        total = None
        for step in range(9):
            for q in range(2):
                term = jnp.dot(
                    window(step // 3, step % 3, q, pl.ds(pair * 2, 2)),
                    weights[step, q * 256:(q + 1) * 256, :],
                    preferred_element_type=F32,
                )
                total = term if total is None else total + term
        total = total.reshape(64, 8, 2 * C)
        both = jnp.stack([total[:, :, :C], total[:, :, C:]], axis=1)
        return both.reshape(2, VOX, C)

    def upper_items(pair, carry):
        found = input_terms(pair)
        for k in range(2):
            i = pair * 2 + k
            taken = foreign(i)
            in_grad[i] = jnp.where(taken, 0.0, found[k]).astype(BF16)
            returned[7 - i] = jnp.where(taken, found[k], 0.0).astype(BF16)
        return carry

    lax.fori_loop(2, 4, upper_items, 0)
    give_back = go([remote(returned, landed, pair_sems, 3, partner)])

    for source in range(16):
        @pl.when(source != xy)
        def _():
            remote(send1.at[source], recv1.at[source], rxy_sems, source, partner).wait_recv()
    recv1[xy] = jnp.zeros((8, 16, C), BF16)
    total = sum1[xy]
    for t in range(16):
        total = total + recv1[t].astype(F32)
    sum1[xy] = total
    send2[...] = total.astype(BF16)
    reduce_z = go([remote(send2.at[(z + t) % 8], recv2.at[t - 1], rz_sems, t, peer_z(t)) for t in range(1, 8)])

    def lower_items(pair, carry):
        in_grad[pl.ds(pair * 2, 2)] = input_terms(pair).astype(BF16)
        return carry

    lax.fori_loop(0, 2, lower_items, 0)
    arrive(give_back)
    place = pltpu.make_async_copy(landed, in_grad.at[pl.ds(8, 4)], store_sem)
    place.start()

    arrive(reduce_z)
    total = sum1[xy, z]
    for t in range(7):
        total = total + recv2[t].astype(F32)
    total = total * (1.0 / math.sqrt(BRICKS * VOX))
    filt_grad_ref[0:16, :] = total[:, 0:64]
    filt_grad_ref[16:27, :] = total[0:11, 64:128]
    place.wait()
    for item in started:
        item.wait_send()
    for target in range(16):
        @pl.when(target != xy)
        def _():
            remote(send1.at[target], recv1.at[target], rxy_sems, target, partner).wait_send()


def on_device(acts, preact, cotangent, filt, counts, neighbors):
    vmem, dma = pltpu.VMEM, pltpu.SemaphoreType.DMA
    any_space = pl.BlockSpec(memory_space=pl.ANY)
    in_smem = pl.BlockSpec(memory_space=pltpu.SMEM)
    in_vmem = pl.BlockSpec(memory_space=pltpu.VMEM)
    out_shape = (
        pltpu.VMEM((SLOTS, VOX, C), BF16),
        pltpu.VMEM((27, 64), F32),
    )
    found = pl.pallas_call(
        kernel,
        out_shape=out_shape,
        in_specs=[in_smem, in_vmem, any_space, any_space, any_space, in_vmem],
        out_specs=(in_vmem, in_vmem),
        scratch_shapes=[
            vmem((SLOTS + 4, VOX, C), BF16),
            vmem((SLOTS, VOX, C), BF16),
            vmem((SLOTS, VOX, C), BF16),
            vmem((4, SLOTS + 1, 8, 8, 8, C), F32),
            vmem((SLOTS, VOX, C), BF16),
            vmem((SLOTS, VOX, C), BF16),
            vmem((SLOTS, 64, C), BF16),
            vmem((2, SLOTS, 64, C), BF16),
            vmem((SLOTS, 27), jnp.int32),
            vmem((SLOTS, 27), jnp.int32),
            vmem((ITEMS, 27), jnp.int32),
            pltpu.SMEM((ITEMS, 27), jnp.int32),
            vmem((3, 2, ITEMS, 10, 32, 2 * C), BF16),
            vmem((2 * C, ITEMS * 256), BF16),
            vmem((9, 512, 256), BF16),
            vmem((3464, C), F32),
            vmem((3464, C), F32),
            vmem((2, 16, 8, 16, C), BF16),
            vmem((2, 16, 8, 16, C), F32),
            vmem((16, 8, 16, C), F32),
            vmem((16, 8, 16, C), F32),
            vmem((16, 8, 16, C), BF16),
            vmem((16, 8, 16, C), BF16),
            vmem((8, 16, C), BF16),
            vmem((7, 16, C), BF16),
            vmem((4, VOX, C), BF16),
            vmem((4, VOX, C), BF16),
            dma((9,)), dma(()), dma(()), dma((2, 8)), dma((2, 2)), dma((2, 8)), dma((2, 16)), dma((2, 1)),
            dma((2, 3)), dma((2, 16)), dma((2, 8)),
        ],
        compiler_params=pltpu.CompilerParams(
            collective_id=0, has_side_effects=True, vmem_limit_bytes=62_000_000
        ),
        name="brick_backward",
    )(counts, neighbors, acts, preact, cotangent, filt)
    return found


def solution(mesh):
    in_specs = (
        P(("space", "rep"), None, None),
        P(("space", "rep"), None, None),
        P(("space", "rep"), None, None),
        P("space", "rep"),
        P(),
        P(("space", "rep"), None),
    )
    out_specs = (P(("space", "rep"), None, None), P("space", "rep"))
    return jax.shard_map(
        on_device, mesh=mesh, in_specs=in_specs, out_specs=out_specs, check_vma=False
    )
```

```python
import math

import jax
import jax.numpy as jnp
from jax import lax
from jax.experimental import pallas as pl
from jax.experimental.pallas import tpu as pltpu
from jax.sharding import PartitionSpec as P


SLOTS = 12
VOX = 512
C = 128
DEVICES = 256
CHIPS = 128
BRICKS = SLOTS * DEVICES
F32 = jnp.float32
BF16 = jnp.bfloat16
MESH = pl.DeviceIdType.MESH
ITEMS = 8


def slope_times(cotangent, preact):
    values = preact.astype(F32)
    sigma = 0.5 + 0.5 * jnp.tanh(0.5 * values)
    return cotangent.astype(F32) * (sigma * (1.0 + values * (1.0 - sigma)))


def kernel(
    counts, neighbors, acts_hbm, pre_hbm, cot_hbm, filt_ref, in_grad, filt_grad_ref,
    acts, pre, cot, grads, own_g, other_g, halo_out, halo_in, own_table, other_table, mixed_table, table, pads, acts_t, weights,
    filt_sum, filt_full, rows, rs_pair, rs_pair_in, sum1, send1, recv1, send2, recv2, returned, landed,
    load_sem, store_sem, table_sem, pair_sems, halo_sems, gz_sems, gxy_sems, gp_sems, rp_sems, rxy_sems, rz_sems,
):
    chip = lax.axis_index("space")
    core = lax.axis_index("rep")
    device = chip * 2 + core
    z = chip % 8
    xy = chip // 8

    def to(chip_id, core_id):
        return {"space": chip_id, "rep": core_id}

    partner = to(chip, 1 - core)

    def peer_xy(t):
        return to((xy + t) % 16 * 8 + z, core)

    def peer_z(t):
        return to(xy * 8 + (z + t) % 8, core)

    def load(source, target, part, index):
        span = pl.ds(part * 4, 4)
        return pltpu.make_async_copy(source.at[span], target.at[span], load_sem.at[index * 3 + part])

    pairs = ((pre_hbm, pre), (cot_hbm, cot), (acts_hbm, acts))
    loads = [load(s, t, part, i) for i, (s, t) in enumerate(pairs) for part in range(3)]
    for item in loads[:6]:
        item.start()

    barrier = pltpu.get_barrier_semaphore()
    facing = to((chip + CHIPS - 1 + 2 * core) % CHIPS, 1 - core)
    greeted = [partner, facing]
    greeted += [peer_z(t) for t in range(1, 8)] + [peer_xy(t) for t in range(1, 16)]
    for other in greeted:
        pl.semaphore_signal(barrier, inc=1, device_id=other, device_id_type=MESH)

    def remote(source, target, sems, index, other, landing=None):
        return pltpu.make_async_remote_copy(
            src_ref=source, dst_ref=target, send_sem=sems.at[0, index],
            recv_sem=sems.at[1, index if landing is None else landing],
            device_id=other, device_id_type=MESH,
        )

    started = []

    def go(copies):
        for item in copies:
            item.start()
        started.extend(copies)
        return copies

    def arrive(copies):
        for item in copies:
            item.wait_recv()

    left = lax.broadcasted_iota(jnp.int32, (1, C), 1) < 64

    def swap(top, bottom):
        return jnp.where(left, top, pltpu.roll(bottom, 64, 1)), jnp.where(left, pltpu.roll(top, 64, 1), bottom)

    filt_sum[0:32, :] = jnp.zeros((32, C), F32)
    filt_sum[0:27, 0:64] = filt_ref[...].astype(F32)
    rows[core, xy, z] = swap(filt_sum[0:16, :], filt_sum[16:32, :])[0].astype(BF16)
    filt_sum[3456:3464, :] = jnp.zeros((8, C), F32)
    empty = jnp.zeros((8, 8, C), F32)
    grads[0, SLOTS, 7] = empty
    grads[3, SLOTS, 0] = empty
    for x in range(8):
        grads[1, SLOTS, x] = empty
        grads[2, SLOTS, x] = empty

    own_count = counts[device]
    other_count = counts[device + 1 - 2 * core]
    tap = lax.broadcasted_iota(jnp.int32, (SLOTS, 27), 1)
    brick = lax.broadcasted_iota(jnp.int32, (SLOTS, 27), 0)
    found = neighbors[...]
    first = (device - 1) * SLOTS + jnp.where(tap >= 9, SLOTS, 0) + jnp.where(tap >= 18, SLOTS, 0)
    own_table[...] = jnp.where(
        (found < BRICKS) & (brick < own_count), jnp.clip(found - first, 0, SLOTS - 1), SLOTS
    )
    for item in loads[:6]:
        item.wait()
    for item in loads[6:]:
        item.start()

    def outer_layer(b, carry):
        span = pl.ds(pl.multiple_of(core * 448, 64), 64)
        g = slope_times(cot[b, span, :], pre[b, span, :])
        grads[1 + core, b, 7 * core] = g.reshape(8, 8, C)
        halo_out[b] = g.astype(BF16)
        own_g[b, span, :] = g.astype(BF16)
        return carry

    lax.fori_loop(0, SLOTS, outer_layer, 0)
    pl.semaphore_wait(barrier, len(greeted))
    here = rows.at[core, xy, z]
    gather_z = go([remote(here, here, gz_sems, t, peer_z(t)) for t in range(1, 8)])
    go([remote(halo_out, halo_in.at[1 - core], halo_sems, 0, facing, 1 - core)])
    swap_table = go([remote(own_table, other_table, pair_sems, 0, partner)])

    def inner_layers(b, carry):
        for j in range(7):
            x = j + 1 - core
            span = pl.ds(pl.multiple_of(x * 64, 64), 64)
            g = slope_times(cot[b, span, :], pre[b, span, :])
            grads[1 + core, b, x] = g.reshape(8, 8, C)
            own_g[b, span, :] = g.astype(BF16)
        return carry

    def foreign(i):
        return (i >= 4) & (15 - i < other_count)

    swap_g = []
    for part in range(3):
        lax.fori_loop(part * 4, part * 4 + 4, inner_layers, 0)
        span = pl.ds(part * 4, 4)
        swap_g += go([remote(own_g.at[span], other_g.at[span], pair_sems, 4 + part, partner)])
        if part == 0:
            arrive(swap_table)
            mixed_table[0:4, :] = own_table[0:4, :]
            for i in range(4, ITEMS):
                mixed_table[i:i + 1, :] = jnp.where(foreign(i), other_table[15 - i:16 - i, :], own_table[i:i + 1, :])
            table_copy = pltpu.make_async_copy(mixed_table, table, table_sem)
            table_copy.start()
    swap_acts = go([remote(acts_hbm.at[pl.ds(8, 4)], acts.at[pl.ds(SLOTS, 4)], pair_sems, 1, partner)])
    for item in loads[6:]:
        item.wait()

    def transpose_acts(i, brick):
        a = acts[brick].astype(F32).reshape(32, 2, 8, C)
        span = pl.ds(pl.multiple_of(i * 256, 256), 256)
        for parity in range(2):
            acts_t[parity * C:(parity + 1) * C, span] = a[:, parity].reshape(256, C).T.astype(BF16)

    def lower_acts(i, carry):
        transpose_acts(i, i)
        return carry

    def upper_acts(i, carry):
        transpose_acts(i, jnp.where(foreign(i), SLOTS + 7 - i, i))
        return carry

    lax.fori_loop(0, 4, lower_acts, 0)
    table_copy.wait()

    row = lax.broadcasted_iota(jnp.int32, (1, 8, C), 1)

    def assemble(i, layer, planes):
        parity = jnp.where(foreign(i), 1 - core, core)
        slots = {(sy, sz): table[i, layer * 9 + (sy + 1) * 3 + sz + 1] for sy in (-1, 0, 1) for sz in (-1, 0, 1)}
        for x_from, count, x_to in planes:
            for lane in range(2):
                tiles = []
                for pair in range(5):
                    padded_y = 2 * pair + lane
                    sy = -1 if padded_y == 0 else 1 if padded_y == 9 else 0
                    y = (padded_y - 1) % 8
                    mid, low, high = (
                        grads[parity + layer, slots[sy, sz], x_from:x_from + count, y] for sz in (0, -1, 1)
                    )
                    tiles.append((
                        pltpu.roll(jnp.where(row == 7, low, mid), 1, 1),
                        mid,
                        pltpu.roll(jnp.where(row == 0, high, mid), 7, 1),
                    ))
                for shift in range(3):
                    for q in range(2):
                        for half in range(2):
                            both = jnp.concatenate(
                                [tiles[q + 2 * half][shift], tiles[q + 2 * half + 1][shift]], axis=1
                            )
                            pads[
                                shift, q, i, x_to:x_to + count, half * 16:(half + 1) * 16, lane * C:(lane + 1) * C
                            ] = both.astype(BF16)

    def assemble_own(i, carry):
        assemble(i, 1, [(x, 2, x + 1) for x in range(0, 8, 2)])
        return carry

    lax.fori_loop(0, 4, assemble_own, 0)
    arrive(swap_g[:2])

    def widen(b, carry):
        grads[2 - core, b] = other_g[b].astype(F32).reshape(8, 8, 8, C)
        return carry

    lax.fori_loop(0, 8, widen, 0)
    arrive(swap_g[2:])
    lax.fori_loop(8, SLOTS, widen, 0)
    lax.fori_loop(4, ITEMS, assemble_own, 0)
    arrive(gather_z)
    here = rows.at[core, xy]
    gather_xy = go([remote(here, here, gxy_sems, t, peer_xy(t)) for t in range(1, 16)])
    arrive(swap_acts)
    lax.fori_loop(4, ITEMS, upper_acts, 0)

    def window(step_x, step_z, q, items):
        found = pads[2 - step_z, q, items, pl.ds(2 - step_x, 8), :, :]
        return found.reshape(found.shape[0] * 256, 256)

    def filter_terms(step_x, step_z, carry):
        lhs = acts_t[...]
        q0, q1 = (
            jnp.dot(lhs, window(step_x, step_z, q, pl.ds(0, ITEMS)), preferred_element_type=F32) for q in range(2)
        )
        for step_y, term in (
            (0, q1[:C, :C] + q1[C:, C:]),
            (1, q0[:C, C:] + q1[C:, :C]),
            (2, q0[:C, :C] + q0[C:, C:]),
        ):
            tap = step_x * 9 + step_y * 3 + step_z
            filt_sum[pl.ds(pl.multiple_of(tap * C, C), C), :] = term
        return carry

    def deal(i, carry):
        block = filt_sum.at[pl.ds(pl.multiple_of(i * 216, 8), 224)]
        for k in range(8):
            rs_pair[0, i, k], rs_pair[1, i, k] = swap(block[27 * k:27 * k + 16], block[27 * k + 16:27 * k + 32])
        return carry

    parts = ((6, 10), (0, 6), (10, 16))

    def post_pair(part):
        low, high = parts[part]
        lax.fori_loop(low, high, deal, 0)
        span = pl.ds(low, high - low)
        return go([remote(rs_pair.at[1 - core, span], rs_pair_in.at[span], rp_sems, part, partner)])

    def add_pair(i, carry):
        total = rs_pair[core, i] + rs_pair_in[i]
        sum1[i] = total
        send1[i] = total.astype(BF16)
        return carry

    def send_on(part, reduce_pair):
        arrive(reduce_pair)
        low, high = parts[part]
        lax.fori_loop(low, high, add_pair, 0)
        for target in range(low, high):
            @pl.when(target != xy)
            def _():
                remote(send1.at[target], recv1.at[xy], rxy_sems, target, to(target * 8 + z, core), xy).start()

    lax.fori_loop(0, 1, lambda step_z, carry: filter_terms(1, step_z, carry), 0)
    remote(halo_out, halo_in.at[core], halo_sems, 0, partner, core).wait_recv()
    go([remote(halo_in.at[core], halo_in.at[core], halo_sems, 1, partner, core)])
    lax.fori_loop(1, 3, lambda step_z, carry: filter_terms(1, step_z, carry), 0, unroll=True)
    reduce_pair = post_pair(0)

    remote(halo_out, halo_in.at[1 - core], halo_sems, 0, partner, 1 - core).wait_recv()

    def widen_halo(b, carry):
        grads[0, b, 7] = halo_in[0, b].astype(F32).reshape(8, 8, C)
        grads[3, b, 0] = halo_in[1, b].astype(F32).reshape(8, 8, C)
        return carry

    lax.fori_loop(0, SLOTS, widen_halo, 0)

    def assemble_halo(i, carry):
        assemble(i, 0, [(7, 1, 0)])
        assemble(i, 2, [(0, 1, 9)])
        return carry

    lax.fori_loop(0, ITEMS, assemble_halo, 0)
    lax.fori_loop(0, 1, lambda step_z, carry: filter_terms(0, step_z, carry), 0)
    send_on(0, reduce_pair)
    lax.fori_loop(1, 3, lambda step_z, carry: filter_terms(0, step_z, carry), 0, unroll=True)
    reduce_pair = post_pair(1)
    lax.fori_loop(0, 2, lambda step_z, carry: filter_terms(2, step_z, carry), 0, unroll=True)
    send_on(1, reduce_pair)
    lax.fori_loop(2, 3, lambda step_z, carry: filter_terms(2, step_z, carry), 0)
    reduce_pair = post_pair(2)
    send_on(2, reduce_pair)
    arrive(gather_xy)
    here = rows.at[core]
    gather_last = go([remote(here, here, gp_sems, 0, partner)])

    arrive(gather_last)

    def undeal(i, carry):
        block = filt_full.at[pl.ds(pl.multiple_of(i * 216, 8), 224)]
        for k in range(8):
            top, bottom = swap(rows[0, i, k].astype(F32), rows[1, i, k].astype(F32))
            block[27 * k:27 * k + 16] = top
            block[27 * k + 16:27 * k + 32] = bottom
        return carry

    lax.fori_loop(0, 16, undeal, 0)

    def build_weights(i, carry):
        step_x, step_z = i // 3, i % 3
        taps = []
        for step_y in range(3):
            tap = step_x * 9 + step_y * 3 + step_z
            taps.append(filt_full[pl.ds(pl.multiple_of(tap * C, C), C), :].T.astype(BF16))
        zero = jnp.zeros((C, C), BF16)
        for q in range(2):
            for lane in range(2):
                for parity in range(2):
                    step_y = parity - (2 * q + lane - 1) + 1
                    block = taps[step_y] if 0 <= step_y <= 2 else zero
                    weights[i, q * 256 + lane * C:q * 256 + (lane + 1) * C, parity * C:(parity + 1) * C] = block
        return carry

    lax.fori_loop(0, 9, build_weights, 0)

    def input_terms(pair):
        total = None
        for step in range(9):
            for q in range(2):
                term = jnp.dot(
                    window(step // 3, step % 3, q, pl.ds(pair * 2, 2)),
                    weights[step, q * 256:(q + 1) * 256, :],
                    preferred_element_type=F32,
                )
                total = term if total is None else total + term
        total = total.reshape(64, 8, 2 * C)
        both = jnp.stack([total[:, :, :C], total[:, :, C:]], axis=1)
        return both.reshape(2, VOX, C)

    def upper_items(pair, carry):
        found = input_terms(pair)
        for k in range(2):
            i = pair * 2 + k
            taken = foreign(i)
            in_grad[i] = jnp.where(taken, 0.0, found[k]).astype(BF16)
            returned[7 - i] = jnp.where(taken, found[k], 0.0).astype(BF16)
        return carry

    lax.fori_loop(2, 4, upper_items, 0)
    give_back = go([remote(returned, landed, pair_sems, 3, partner)])

    for source in range(16):
        @pl.when(source != xy)
        def _():
            remote(send1.at[source], recv1.at[source], rxy_sems, source, partner).wait_recv()
    recv1[xy] = jnp.zeros((8, 16, C), BF16)
    total = sum1[xy]
    for t in range(16):
        total = total + recv1[t].astype(F32)
    sum1[xy] = total
    send2[...] = total.astype(BF16)
    reduce_z = go([remote(send2.at[(z + t) % 8], recv2.at[t - 1], rz_sems, t, peer_z(t)) for t in range(1, 8)])

    def lower_items(pair, carry):
        in_grad[pl.ds(pair * 2, 2)] = input_terms(pair).astype(BF16)
        return carry

    lax.fori_loop(0, 2, lower_items, 0)
    arrive(give_back)
    place = pltpu.make_async_copy(landed, in_grad.at[pl.ds(8, 4)], store_sem)
    place.start()

    arrive(reduce_z)
    total = sum1[xy, z]
    for t in range(7):
        total = total + recv2[t].astype(F32)
    total = total * (1.0 / math.sqrt(BRICKS * VOX))
    filt_grad_ref[0:16, :] = total[:, 0:64]
    filt_grad_ref[16:27, :] = total[0:11, 64:128]
    place.wait()
    for item in started:
        item.wait_send()
    for target in range(16):
        @pl.when(target != xy)
        def _():
            remote(send1.at[target], recv1.at[target], rxy_sems, target, partner).wait_send()


def on_device(acts, preact, cotangent, filt, counts, neighbors):
    vmem, dma = pltpu.VMEM, pltpu.SemaphoreType.DMA
    any_space = pl.BlockSpec(memory_space=pl.ANY)
    in_smem = pl.BlockSpec(memory_space=pltpu.SMEM)
    in_vmem = pl.BlockSpec(memory_space=pltpu.VMEM)
    out_shape = (
        pltpu.VMEM((SLOTS, VOX, C), BF16),
        pltpu.VMEM((27, 64), F32),
    )
    found = pl.pallas_call(
        kernel,
        out_shape=out_shape,
        in_specs=[in_smem, in_vmem, any_space, any_space, any_space, in_vmem],
        out_specs=(in_vmem, in_vmem),
        scratch_shapes=[
            vmem((SLOTS + 4, VOX, C), BF16),
            vmem((SLOTS, VOX, C), BF16),
            vmem((SLOTS, VOX, C), BF16),
            vmem((4, SLOTS + 1, 8, 8, 8, C), F32),
            vmem((SLOTS, VOX, C), BF16),
            vmem((SLOTS, VOX, C), BF16),
            vmem((SLOTS, 64, C), BF16),
            vmem((2, SLOTS, 64, C), BF16),
            vmem((SLOTS, 27), jnp.int32),
            vmem((SLOTS, 27), jnp.int32),
            vmem((ITEMS, 27), jnp.int32),
            pltpu.SMEM((ITEMS, 27), jnp.int32),
            vmem((3, 2, ITEMS, 10, 32, 2 * C), BF16),
            vmem((2 * C, ITEMS * 256), BF16),
            vmem((9, 512, 256), BF16),
            vmem((3464, C), F32),
            vmem((3464, C), F32),
            vmem((2, 16, 8, 16, C), BF16),
            vmem((2, 16, 8, 16, C), F32),
            vmem((16, 8, 16, C), F32),
            vmem((16, 8, 16, C), F32),
            vmem((16, 8, 16, C), BF16),
            vmem((16, 8, 16, C), BF16),
            vmem((8, 16, C), BF16),
            vmem((7, 16, C), BF16),
            vmem((4, VOX, C), BF16),
            vmem((4, VOX, C), BF16),
            dma((9,)), dma(()), dma(()), dma((2, 8)), dma((2, 2)), dma((2, 8)), dma((2, 16)), dma((2, 1)),
            dma((2, 3)), dma((2, 16)), dma((2, 8)),
        ],
        compiler_params=pltpu.CompilerParams(
            collective_id=0, has_side_effects=True, vmem_limit_bytes=62_000_000
        ),
        name="brick_backward",
    )(counts, neighbors, acts, preact, cotangent, filt)
    return found


def solution(mesh):
    in_specs = (
        P(("space", "rep"), None, None),
        P(("space", "rep"), None, None),
        P(("space", "rep"), None, None),
        P("space", "rep"),
        P(),
        P(("space", "rep"), None),
    )
    out_specs = (P(("space", "rep"), None, None), P("space", "rep"))
    return jax.shard_map(
        on_device, mesh=mesh, in_specs=in_specs, out_specs=out_specs, check_vma=False
    )
```
